512 devices in a mesh: ctx: 64 (over z, x), head: 8 (over y, core).
Axes of the slice: x: 4, y: 4, z: 16, core: 2. Of those that a mesh axis runs over, the one named last changes fastest.
Arguments:
- queries: bfloat16 [16384, 4096], P('ctx', 'head'), may hold values from -4.5 to 4.5
- keys: bfloat16 [16384, 1024], P('ctx', 'head'), may hold values from -4.5 to 4.5
- values: bfloat16 [16384, 1024], P('ctx', 'head'), may hold values from -6 to 6
- out_weight: bfloat16 [4096, 4096], P('head'), may hold values from -0.125 to 0.125
- doc_blocks: int32 [4], replicated, may hold values from 1 to 64, 128 in all
- swap_pairs: int32 [128], replicated, may hold values from 0 to 127, as said below
Outputs:
- mixed: bfloat16 [16384, 4096], P('ctx', 'head')
The draws below stay inside these ranges and needn't reach their ends.
Inputs may be any that keep to these rules, and one draw needn't show every extreme that they name: swap_pairs[b] is the sequence block held in stored block b (rows b * 128 to b * 128 + 127); the 128 blocks are paired in swaps: swap_pairs[swap_pairs[b]] = b and swap_pairs[b] != b. `doc_blocks`: the lengths sum to 128.
All inputs are finite; a program needn't handle non-finite values.
Results may differ from the reference program's by a relative error of at most 0.018.
Values may be sent and summed in bfloat16 or wider, within the bound.
A program may use at most 64 MiB of HBM per device.

```python
import math
import jax
import jax.numpy as jnp
import numpy as np
from jax import lax

D = 4096
QH = 32
KVH = 8
HD = 128
BLOCK = 128
NB = 128
MOST = 64
TOKENS = 16384
DOCS = 4
N_HEAD = 8


def draw_pair(key):
    row_count = TOKENS
    kv_width = KVH * HD
    query_rows = jnp.clip(jax.random.normal(jax.random.fold_in(key, 21), (row_count, QH * HD), jnp.float32), -4.5, 4.5)
    key_rows = jnp.clip(jax.random.normal(jax.random.fold_in(key, 22), (row_count, kv_width), jnp.float32), -4.5, 4.5)
    return (query_rows, key_rows)


def draw_queries(key, part):
    return draw_pair(key)[0].astype(jnp.bfloat16)


def draw_keys(key, part):
    return draw_pair(key)[1].astype(jnp.bfloat16)


def draw_swap_pairs(key, part):
    shuffled = jax.random.permutation(jax.random.fold_in(key, 31), NB).astype(jnp.int32)
    paired = jnp.zeros((NB,), jnp.int32)
    paired = paired.at[shuffled[0::2]].set(shuffled[1::2])
    paired = paired.at[shuffled[1::2]].set(shuffled[0::2])
    return paired


def with_spikes(entries, rng, source, target, shards_of, factor):
    owner, partner = [(jnp.arange(entries.shape[axis_at]) // (entries.shape[axis_at] // shards_of)).reshape([-1 if axis == axis_at else 1 for axis in range(entries.ndim)]) for axis_at in (source, target)]
    chosen = jax.random.permutation(rng, shards_of)[partner]
    strong = (owner == chosen) | (owner == (partner + shards_of // 2) % shards_of)
    return jnp.where(strong, factor * entries, entries)


def steps_of(key, dims, shards, smallest, top_value):
    loudness, own = 1.0, jax.random.fold_in(key, 6)
    for position, parts in shards:
        steps = jnp.exp(jax.random.uniform(jax.random.fold_in(own, position), (parts,), jnp.float32, smallest / len(shards), top_value / len(shards)))
        loudness = loudness * jnp.repeat(steps, dims[position] // parts).reshape([-1 if axis == position else 1 for axis in range(len(dims))])
    return loudness


def length_profile(number_of, total, most, lean):
    loads = [(1 << 20) // math.isqrt(grade ** lean) + 1 for grade in range(2, number_of + 1)]
    spare, given = total - most - (number_of - 1), [1] * (number_of - 1)
    while spare > 0:
        movable = [i for i in range(number_of - 1) if given[i] < most]
        mass, left = sum([loads[i] for i in movable]), spare
        for i in movable:
            extra = min(most - given[i], max(1, left * loads[i] // mass), spare)
            given[i] = given[i] + extra
            spare = spare - extra
    return np.array([most] + given)


def uneven(own_key, number_of, total, reach, slope):
    if number_of == 2:
        one = jax.random.randint(own_key, (), max(1, total - reach), min(reach, total - 1) + 1)
        return jnp.stack([one, total - one])
    sizes = jnp.asarray(length_profile(number_of, total, reach, slope), jnp.int32)
    couples = (number_of - 1) // 2
    donor, sink = sizes[1:1 + 2 * couples:2], sizes[2:2 + 2 * couples:2]
    slack = jnp.minimum(donor - 1, reach - sink)
    moved = jax.random.randint(jax.random.fold_in(own_key, 1), (couples,), 0, 1 << 20) % (slack + 1)
    sizes = sizes.at[1:1 + 2 * couples:2].set(donor - moved).at[2:2 + 2 * couples:2].set(sink + moved)
    return sizes[jax.random.permutation(jax.random.fold_in(own_key, 2), number_of)]


def bell_draw(rng, dims, deviation, most, pieces=(), kind=jnp.bfloat16):
    result = deviation * jax.random.normal(rng, dims, jnp.float32)
    if pieces:
        result = result * steps_of(rng, dims, pieces, -0.22, 0.18)
    return jnp.clip(result, -most, most).astype(kind)


def bell_draw_with(own_key, dims, width, reach, cuts, heavy, kind=jnp.bfloat16):
    values = width * jax.random.normal(own_key, dims, jnp.float32)
    if cuts:
        values = values * steps_of(own_key, dims, cuts, -0.22, 0.18)
    return jnp.clip(with_spikes(values, jax.random.fold_in(own_key, 3), *heavy), -reach, reach).astype(kind)


def setup_inputs(seed: int = 0) -> dict:
    seeds = jax.random.split(jax.random.key(seed), 7)
    return {
        "queries": draw_queries(jax.random.fold_in(seeds[6], 71), 0),
        "keys": draw_keys(jax.random.fold_in(seeds[6], 71), 0),
        "values": bell_draw(seeds[2], (TOKENS, KVH * HD), 1.0, 6.0, ((0, 64), (1, 8))),
        "out_weight": bell_draw_with(seeds[3], (QH * HD, D), (QH * HD) ** -0.5, 0.125, ((0, 8),), (0, 1, 8, 2.0)),
        "doc_blocks": uneven(seeds[4], DOCS, NB, MOST, 2).astype(jnp.int32),
        "swap_pairs": draw_swap_pairs(jax.random.fold_in(seeds[6], 71), 0),
    }


masked_score = -1.0e30


def reference(queries, keys, values, out_weight, doc_blocks, swap_pairs):
    group_size = QH // KVH
    window_rows = MOST * BLOCK
    doc_ends = jnp.cumsum(doc_blocks).astype(jnp.int32)
    seq_ids = jnp.arange(NB, dtype=jnp.int32)
    doc_of_seq = jnp.sum((doc_ends[None, :] <= seq_ids[:, None]).astype(jnp.int32), axis=1).astype(jnp.int32)
    inverse = jnp.zeros((NB,), jnp.int32).at[swap_pairs.astype(jnp.int32)].set(seq_ids)
    key_rows = keys.reshape(NB, BLOCK, KVH, HD)[inverse].reshape(TOKENS, KVH, HD).astype(jnp.float32)
    value_rows = values.reshape(NB, BLOCK, KVH, HD)[inverse].reshape(TOKENS, KVH, HD).astype(jnp.float32)
    padding_rows = window_rows - BLOCK
    key_rows = jnp.concatenate([jnp.zeros((padding_rows, KVH, HD), jnp.float32), key_rows], axis=0)
    value_rows = jnp.concatenate([jnp.zeros((padding_rows, KVH, HD), jnp.float32), value_rows], axis=0)
    seq_doc = jnp.repeat(doc_of_seq, BLOCK).astype(jnp.int32)
    seq_doc = jnp.concatenate([jnp.full((padding_rows,), -1, jnp.int32), seq_doc], axis=0)
    seq_pos = jnp.arange(TOKENS, dtype=jnp.int32)
    seq_pos = jnp.concatenate([jnp.full((padding_rows,), -1, jnp.int32), seq_pos], axis=0)
    query_blocks = queries.reshape(NB, BLOCK, KVH, group_size, HD)
    score_scale = HD ** -0.5
    offsets = jnp.arange(BLOCK, dtype=jnp.int32)

    def one_block(inputs_block):
        block_queries, seq_block = inputs_block
        query_pos = (seq_block * BLOCK + offsets).astype(jnp.int32)
        query_doc = doc_of_seq[seq_block]
        begin = (seq_block * BLOCK).astype(jnp.int32)
        window_keys = lax.dynamic_slice_in_dim(key_rows, begin, window_rows, 0)
        window_values = lax.dynamic_slice_in_dim(value_rows, begin, window_rows, 0)
        window_doc = lax.dynamic_slice_in_dim(seq_doc, begin, window_rows, 0)
        window_pos = lax.dynamic_slice_in_dim(seq_pos, begin, window_rows, 0)
        scores = jnp.einsum("rkgd,skd->kgrs", block_queries.astype(jnp.float32), window_keys, precision=lax.Precision.HIGHEST) * score_scale
        visible = (window_doc[None, :] == query_doc) & (window_pos[None, :] <= query_pos[:, None])
        scores = jnp.where(visible[None, None], scores, masked_score)
        row_max = jnp.max(scores, axis=-1, keepdims=True)
        lifted = jnp.where(visible[None, None], jnp.exp(scores - row_max), 0.0)
        denominator = jnp.sum(lifted, axis=-1)
        weights = lax.optimization_barrier(lifted.astype(jnp.bfloat16)).astype(jnp.float32)
        summed = jnp.einsum("kgrs,skd->rkgd", weights, window_values, precision=lax.Precision.HIGHEST)
        return (summed / jnp.transpose(denominator, (2, 0, 1))[..., None]).astype(jnp.bfloat16)

    attended = lax.map(one_block, (query_blocks, swap_pairs.astype(jnp.int32)))
    attended = attended.reshape(TOKENS, QH * HD)
    group_rows = QH * HD // N_HEAD
    mixed = jnp.zeros((TOKENS, D), jnp.float32)
    for member in range(N_HEAD):
        partial_value = jnp.dot(attended[:, member * group_rows:(member + 1) * group_rows], out_weight[member * group_rows:(member + 1) * group_rows], preferred_element_type=jnp.float32)
        rounded = lax.optimization_barrier(partial_value.astype(jnp.bfloat16))
        mixed = mixed + rounded.astype(jnp.float32)
    return mixed.astype(jnp.bfloat16)
```

```python
import functools

import jax
import jax.numpy as jnp
from jax import lax
from jax.experimental import pallas as pl
from jax.experimental.pallas import tpu as pltpu
from jax.sharding import PartitionSpec as P

HD = 128
BLOCK = 128
NX = 4
NC = 2
SCALE2 = 1.4426950408889634 * HD ** (-0.5)
MASKED = -1e30
MESH = pl.DeviceIdType.MESH
ANY = pl.BlockSpec(memory_space=pl.ANY)
VMEM = pl.BlockSpec(memory_space=pltpu.VMEM)
SMEM = pl.BlockSpec(memory_space=pltpu.SMEM)


def remote(src, dst, send_sem, recv_sem, device):
    return pltpu.make_async_remote_copy(
        src_ref=src,
        dst_ref=dst,
        send_sem=send_sem,
        recv_sem=recv_sem,
        device_id=device,
        device_id_type=MESH,
    )


def greet(devices):
    barrier = pltpu.get_barrier_semaphore()
    for device in devices:
        pl.semaphore_signal(barrier, inc=1, device_id=device, device_id_type=MESH)
    pl.semaphore_wait(barrier, len(devices))


def gather_kernel(nz, q_ref, k_ref, v_ref, q_all, k_all, v_all, vt, ksend, krecv, vsend, vrecv, qsend, qrecv, local_sem):
    ctx = lax.axis_index("ctx")
    head = lax.axis_index("head")
    z, x = ctx // NX, lax.rem(ctx, NX)
    at = lambda zz, xx: (lax.rem(zz + nz, nz) * NX + lax.rem(xx + NX, NX), head)
    up, down = at(z + 1, x), at(z - 1, x)
    right, left = at(z, x + 1), at(z, x - 1)
    vt[...] = v_ref[...].T
    greet([up, down, right, left])
    half = q_ref.shape[0] // 2
    qpart = lambda ref, part: ref.at[pl.ds(part * half, half)]

    def zcopy(array, sends, recvs, own, step, way):
        origin = lax.rem(z - step + nz, nz) if way == 0 else lax.rem(z + step, nz)
        src = own if step == 0 else array.at[origin]
        return remote(
            src, array.at[origin], sends.at[way, step], recvs.at[way, step], up if way == 0 else down
        )

    far = nz // 2
    kc = [[zcopy(k_all, ksend, krecv, k_ref, s, w) for s in range(far if w == 0 else far - 1)] for w in (0, 1)]
    vc = [[zcopy(v_all, vsend, vrecv, vt, s, w) for s in range(far - 1 if w == 0 else far)] for w in (0, 1)]
    for w in (0, 1):
        kc[w][0].start()
    for w in (0, 1):
        vc[w][0].start()

    def qcopy(way, part):
        return remote(
            qpart(q_ref, part), qpart(q_all.at[x], part), qsend.at[way, part], qrecv.at[way, part],
            right if way == 0 else left,
        )

    qc = [[qcopy(0, 0), qcopy(0, 1)], [qcopy(1, 1), qcopy(1, 0)]]
    for i in (0, 1):
        for w in (0, 1):
            qc[w][i].start()
    local = [
        pltpu.make_async_copy(q_ref, q_all.at[x], local_sem.at[0]),
        pltpu.make_async_copy(k_ref, k_all.at[z], local_sem.at[1]),
        pltpu.make_async_copy(vt, v_all.at[z], local_sem.at[2]),
    ]
    for c in local:
        c.start()

    qx = []
    for step in range(far):
        for copies in (kc, vc):
            for w in (0, 1):
                if step < len(copies[w]):
                    copies[w][step].wait_recv()
                    if step + 1 < len(copies[w]):
                        copies[w][step + 1].start()
        if step == 2:
            origins = (lax.rem(x + NX - 1, NX), lax.rem(x + 1, NX))
            for w in (0, 1):
                qc[w][0].wait_recv()
                c = remote(
                    qpart(q_all.at[origins[w]], w), qpart(q_all.at[origins[w]], w),
                    qsend.at[w, 2], qrecv.at[w, 2], right if w == 0 else left,
                )
                c.start()
                qx.append(c)
    for w in (0, 1):
        qc[w][1].wait_recv()
        qx[w].wait_recv()
    for w in (0, 1):
        for c in kc[w] + vc[w] + qc[w] + [qx[w]]:
            c.wait_send()
    for c in local:
        c.wait()


def attend_kernel(nz, swap, docs, q_all, k_all, v_all, o_ref, lse_ref, qt, acc, found):
    ctx = lax.axis_index("ctx")
    z, x = ctx // NX, lax.rem(ctx, NX)
    group = o_ref.shape[1] // HD
    wide = group * BLOCK
    per = q_all.shape[1] // BLOCK
    ndocs = docs.shape[0]
    diff = lax.broadcasted_iota(jnp.int32, (BLOCK, wide), 0) - lax.rem(
        lax.broadcasted_iota(jnp.int32, (BLOCK, wide), 1), BLOCK
    )

    def one_block(qb, _):
        p, t = qb // per, lax.rem(qb, per)
        seq = swap[(z * NX + p) * per + t]
        start = jnp.int32(0)
        end = jnp.int32(0)
        for d in range(ndocs):
            end = end + docs[d]
            start = jnp.where(end <= seq, end, start)

        def look(j, n):
            ks = swap[((j // per) * NX + x) * per + lax.rem(j, per)]
            found[n] = j
            found[64 + n] = (seq - ks) * BLOCK
            return n + ((ks >= start) & (ks <= seq)).astype(jnp.int32)

        count = lax.fori_loop(0, nz * per, look, jnp.int32(0), unroll=4)
        found[count] = jnp.int32(0)
        found[64 + count] = jnp.int32(-(1 << 24))

        rows = pl.ds(pl.multiple_of(t * BLOCK, BLOCK), BLOCK)
        for h in range(group):
            qt[:, h * BLOCK:(h + 1) * BLOCK] = q_all[p, rows, h * HD:(h + 1) * HD].T
        acc[...] = jnp.zeros_like(acc)

        def turn(i, state):
            m, l = state
            scores, vals = [], []
            for e in range(2):
                j = found[2 * i + e]
                limit = found[64 + 2 * i + e]
                piece = pl.ds(pl.multiple_of(lax.rem(j, per) * BLOCK, BLOCK), BLOCK)
                s = jnp.dot(k_all[j // per, piece, :], qt[...], preferred_element_type=jnp.float32)
                scores.append(jnp.where(diff <= limit, s, MASKED))
                vals.append(v_all[j // per, :, piece])
            s = jnp.concatenate(scores, axis=0)
            new = jnp.maximum(m, jnp.max(s, axis=0, keepdims=True))
            shrink = jnp.exp2((m - new) * SCALE2)
            lifted = jnp.exp2((s - new) * SCALE2)
            l = l * shrink + jnp.sum(lifted, axis=0, keepdims=True)
            acc[...] = acc[...] * shrink + jnp.dot(
                jnp.concatenate(vals, axis=1), lifted.astype(jnp.bfloat16), preferred_element_type=jnp.float32
            )
            return new, l

        m, l = lax.fori_loop(
            0, (count + 1) // 2, turn,
            (jnp.full((1, wide), MASKED, jnp.float32), jnp.zeros((1, wide), jnp.float32)),
        )
        some = l > 0.0
        l = jnp.where(some, l, 1.0)
        lse = jnp.where(some, m * SCALE2 + jnp.log2(l), MASKED)
        out = (acc[...] / l).astype(o_ref.dtype)
        for h in range(group):
            o_ref[p, h * HD:(h + 1) * HD, rows] = out[:, h * BLOCK:(h + 1) * BLOCK]
            lse_ref[p, pl.ds(h, 1), rows] = lse[:, h * BLOCK:(h + 1) * BLOCK]
        return 0

    lax.fori_loop(0, NX * per, one_block, 0)


def mix_kernel(
    ny, o_ref, lse_ref, w_ref, out_ref,
    parts, stats, onward, att, given, taken, sums, halves, finals,
    osend, orecv, ssend, srecv, csend, crecv, hsend, hrecv, fsend, frecv,
):
    ctx = lax.axis_index("ctx")
    head = lax.axis_index("head")
    z, x = ctx // NX, lax.rem(ctx, NX)
    y, core = head // NC, lax.rem(head, NC)
    xat = lambda xx: (z * NX + lax.rem(xx + NX, NX), head)
    yat = lambda yy: (ctx, lax.rem(yy + ny, ny) * NC + core)
    right, left, across = xat(x + 1), xat(x - 1), xat(x + 2)
    up, down = yat(y + 1), yat(y - 1)
    twin = (ctx, y * NC + 1 - core)
    greet([right, left, across, up, down, twin])
    xs = [lax.rem(x + 1, NX), lax.rem(x + NX - 1, NX), lax.rem(x + 2, NX)]
    feats, toks = o_ref.shape[1], o_ref.shape[2]
    half = feats // 2
    fpart = lambda ref, part: ref.at[pl.ds(part * half, half)]
    ways = (right, left)

    first = [remote(fpart(o_ref.at[xs[2]], w), onward.at[w], osend.at[2 + w], orecv.at[2 + w], ways[w]) for w in (0, 1)]
    near = [remote(o_ref.at[xs[w]], parts.at[w], osend.at[w], orecv.at[w], ways[w]) for w in (0, 1)]
    small = [
        remote(lse_ref.at[xs[i]], stats.at[i], ssend.at[i], srecv.at[i], (right, left, across)[i]) for i in range(3)
    ]
    for c in small + first + near:
        c.start()
    second = [
        remote(onward.at[w], fpart(parts.at[2], w), osend.at[4 + w], orecv.at[4 + w], ways[w]) for w in (0, 1)
    ]
    for w in (0, 1):
        first[w].wait_recv()
        second[w].start()
    for c in small:
        c.wait_recv()
    own_lse = lse_ref[x]
    lses = [own_lse] + [stats[i] for i in range(3)]
    top = functools.reduce(jnp.maximum, lses)
    shares = [jnp.exp2(v - top) for v in lses]
    total = functools.reduce(jnp.add, shares)
    shares = [v / total for v in shares]
    for c in near:
        c.wait_recv()
    for c in second:
        c.wait_recv()
    for h in range(feats // HD):
        rows = slice(h * HD, (h + 1) * HD)
        mixed = o_ref[x, rows, :].astype(jnp.float32) * shares[0][h:h + 1, :]
        for i in range(3):
            mixed = mixed + parts[i, rows, :].astype(jnp.float32) * shares[1 + i][h:h + 1, :]
        att[:, rows] = mixed.T.astype(jnp.bfloat16)

    cols = out_ref.shape[1]

    def product(yy, cc):
        at = pl.multiple_of((lax.rem(yy + ny, ny) * NC + cc) * cols, cols)
        return jnp.dot(att[...], w_ref[:, pl.ds(at, cols)], preferred_element_type=jnp.float32)

    order = (y + 2, y + 1, y - 1, y)
    twins = []
    for i, yy in enumerate(order):
        given[i] = product(yy, 1 - core).astype(jnp.bfloat16)
        c = remote(given.at[i], taken.at[i], csend.at[i], crecv.at[i], twin)
        c.start()
        twins.append(c)
    tok_half = toks // 2
    tpart = lambda ref, part: ref.at[pl.ds(part * tok_half, tok_half)]
    yways = (up, down)
    hops, lasts = [], []
    for i, yy in enumerate(order):
        mine = product(yy, core)
        twins[i].wait_recv()
        mine = mine + taken[i].astype(jnp.float32)
        if i == 0:
            sums[0] = mine.astype(jnp.bfloat16)
            for w in (0, 1):
                c = remote(tpart(sums.at[0], w), halves.at[w], hsend.at[w], hrecv.at[w], yways[w])
                c.start()
                hops.append(c)
        elif i < 3:
            w = i - 1
            hops[w].wait_recv()
            if w == 0:
                sums[i, :tok_half] = (mine[:tok_half] + halves[w].astype(jnp.float32)).astype(jnp.bfloat16)
                sums[i, tok_half:] = mine[tok_half:].astype(jnp.bfloat16)
            else:
                sums[i, :tok_half] = mine[:tok_half].astype(jnp.bfloat16)
                sums[i, tok_half:] = (mine[tok_half:] + halves[w].astype(jnp.float32)).astype(jnp.bfloat16)
            c = remote(sums.at[i], finals.at[w], fsend.at[w], frecv.at[w], yways[w])
            c.start()
            lasts.append(c)
        else:
            for c in lasts:
                c.wait_recv()
            out_ref[...] = (mine + finals[0].astype(jnp.float32) + finals[1].astype(jnp.float32)).astype(out_ref.dtype)
    for c in small + first + near + second + twins + hops + lasts:
        c.wait_send()


def local(queries, keys, values, out_weight, doc_blocks, swap_pairs, nz, ny):
    toks, feats = queries.shape
    dma = pltpu.SemaphoreType.DMA
    bf = jnp.bfloat16
    far = nz // 2
    q_all, k_all, v_all = pl.pallas_call(
        functools.partial(gather_kernel, nz),
        out_shape=(
            jax.ShapeDtypeStruct((NX, toks, feats), bf),
            jax.ShapeDtypeStruct((nz, toks, HD), bf),
            jax.ShapeDtypeStruct((nz, HD, toks), bf),
        ),
        in_specs=[ANY, ANY, VMEM],
        out_specs=(ANY, ANY, ANY),
        scratch_shapes=[
            pltpu.VMEM((HD, toks), bf),
            dma((2, far)), dma((2, far)), dma((2, far)), dma((2, far)),
            dma((2, 3)), dma((2, 3)), dma((3,)),
        ],
        compiler_params=pltpu.CompilerParams(collective_id=0, has_side_effects=True),
        name="gather",
    )(queries, keys, values)

    partial, lse = pl.pallas_call(
        functools.partial(attend_kernel, nz),
        out_shape=(
            jax.ShapeDtypeStruct((NX, feats, toks), bf),
            jax.ShapeDtypeStruct((NX, 8, toks), jnp.float32),
        ),
        in_specs=[SMEM, SMEM, VMEM, VMEM, VMEM],
        out_specs=(VMEM, VMEM),
        scratch_shapes=[
            pltpu.VMEM((HD, feats), bf),
            pltpu.VMEM((HD, feats), jnp.float32),
            pltpu.SMEM((128,), jnp.int32),
        ],
        compiler_params=pltpu.CompilerParams(vmem_limit_bytes=40 << 20),
        name="attend",
    )(swap_pairs, doc_blocks, q_all, k_all, v_all)

    cols = out_weight.shape[1] // (ny * NC)
    return pl.pallas_call(
        functools.partial(mix_kernel, ny),
        out_shape=jax.ShapeDtypeStruct((toks, cols), bf),
        in_specs=[VMEM, VMEM, VMEM],
        out_specs=VMEM,
        scratch_shapes=[
            pltpu.VMEM((3, feats, toks), bf),
            pltpu.VMEM((3, 8, toks), jnp.float32),
            pltpu.VMEM((2, feats // 2, toks), bf),
            pltpu.VMEM((toks, feats), bf),
            pltpu.VMEM((4, toks, cols), bf),
            pltpu.VMEM((4, toks, cols), bf),
            pltpu.VMEM((3, toks, cols), bf),
            pltpu.VMEM((2, toks // 2, cols), bf),
            pltpu.VMEM((2, toks, cols), bf),
            dma((6,)), dma((6,)), dma((3,)), dma((3,)), dma((4,)), dma((4,)),
            dma((2,)), dma((2,)), dma((2,)), dma((2,)),
        ],
        compiler_params=pltpu.CompilerParams(
            collective_id=1, has_side_effects=True, vmem_limit_bytes=48 << 20
        ),
        name="mix",
    )(partial, lse, out_weight)


def solution(mesh):
    nz = mesh.shape["ctx"] // NX
    ny = mesh.shape["head"] // NC
    in_specs = (P("ctx", "head"), P("ctx", "head"), P("ctx", "head"), P("head", None), P(), P())
    return jax.shard_map(
        functools.partial(local, nz=nz, ny=ny),
        mesh=mesh, in_specs=in_specs, out_specs=P("ctx", "head"), check_vma=False,
    )
```

```python
import functools

import jax
import jax.numpy as jnp
from jax import lax
from jax.experimental import pallas as pl
from jax.experimental.pallas import tpu as pltpu
from jax.sharding import PartitionSpec as P

HD = 128
BLOCK = 128
NX = 4
NC = 2
PER = 2
ONES = 16
SCALE2 = 1.4426950408889634 * HD ** (-0.5)
MASKED = -1e30
MESH = pl.DeviceIdType.MESH
ANY = pl.BlockSpec(memory_space=pl.ANY)
VMEM = pl.BlockSpec(memory_space=pltpu.VMEM)
SMEM = pl.BlockSpec(memory_space=pltpu.SMEM)


def layer_kernel(
    nz, ny,
    swap, docs, q_ref, k_ref, v_ref, w_ref, out_ref,
    q_in, v_in, w_all, k_all, v_all, qt, acc, tops,
    o_give, o_take, s_give, s_take, att, given, taken, sums, finals,
    lsem, zsend, zrecv, vsend, vrecv, ksend, krecv, qsend, qrecv,
    osend, orecv, ssend, srecv, csend, crecv, ysend, yrecv,
):
    ctx = lax.axis_index("ctx")
    head = lax.axis_index("head")
    z, x = ctx // NX, lax.rem(ctx, NX)
    y, core = head // NC, lax.rem(head, NC)
    xk = NX - 1 - x
    xq = x + 1 - 2 * lax.rem(x, 2)
    zat = lambda zz: lax.rem(zz + nz, nz)
    yat = lambda yy: lax.rem(yy + ny, ny)
    up = (zat(z + 1) * NX + x, head)
    down = (zat(z - 1) * NX + x, head)
    key_mate = (z * NX + xk, head)
    query_mate = (z * NX + xq, head)
    twin = (ctx, y * NC + 1 - core)
    ydev = lambda yy: (ctx, yat(yy) * NC + core)
    hops = (2, 1, 3)
    far = nz // 2
    group = qt.shape[2] // BLOCK
    cols = out_ref.shape[1]

    def remote(src, dst, send_sem, recv_sem, device):
        return pltpu.make_async_remote_copy(
            src_ref=src, dst_ref=dst, send_sem=send_sem, recv_sem=recv_sem, device_id=device, device_id_type=MESH
        )

    barrier = pltpu.get_barrier_semaphore()
    friends = [up, down, key_mate, query_mate, twin] + [ydev(y + d) for d in hops]
    for device in friends:
        pl.semaphore_signal(barrier, inc=1, device_id=device, device_id_type=MESH)

    loads = [
        pltpu.make_async_copy(v_ref, v_in, lsem.at[0]),
        pltpu.make_async_copy(q_ref, q_in, lsem.at[1]),
        pltpu.make_async_copy(k_ref, k_all.at[z, 0], lsem.at[2]),
        pltpu.make_async_copy(w_ref, w_all, lsem.at[3]),
    ]
    for c in loads:
        c.start()
    loads[0].wait()
    v_all[z, 0] = v_in[...].T
    loads[1].wait()
    for t in range(PER):
        for h in range(group):
            qt[t, :, h * BLOCK:(h + 1) * BLOCK] = q_in[t * BLOCK:(t + 1) * BLOCK, h * HD:(h + 1) * HD].T
    loads[2].wait()
    pl.semaphore_wait(barrier, len(friends))

    def zcopy(stream, way, step):
        origin = zat(z - step) if way == 0 else zat(z + step)
        ref = v_all.at[origin, 0] if stream == 0 else k_all.at[origin, stream - 1]
        return remote(ref, ref, zsend.at[stream, way, step], zrecv.at[stream, way, step], up if way == 0 else down)

    def vcopy(slot, origin):
        return remote(v_all.at[origin, 0], v_all.at[origin, 1], vsend.at[slot], vrecv.at[slot], key_mate)

    kmate = remote(k_all.at[z, 0], k_all.at[z, 1], ksend, krecv, key_mate)
    qmate = [remote(qt.at[t], qt.at[PER + t], qsend.at[t], qrecv.at[t], query_mate) for t in range(PER)]
    vown = vcopy(2 * far, z)
    kmate.start()
    for stream in (0, 1):
        for way in (0, 1):
            zcopy(stream, way, 0).start()
    for c in qmate:
        c.start()
    vown.start()

    seqs, starts = [], []
    for j in range(2 * PER):
        seq = swap[(z * NX + (x if j < PER else xq)) * PER + j % PER]
        start = jnp.int32(0)
        end = jnp.int32(0)
        for d in range(docs.shape[0]):
            end = end + docs[d]
            start = jnp.where(end <= seq, end, start)
        seqs.append(seq)
        starts.append(start)

    acc[...] = jnp.zeros_like(acc)
    tops[...] = jnp.full_like(tops, MASKED)
    wide = group * BLOCK
    causal = lax.broadcasted_iota(jnp.int32, (BLOCK, wide), 0) <= lax.rem(
        lax.broadcasted_iota(jnp.int32, (BLOCK, wide), 1), BLOCK
    )

    def absorb(j, chunks, diagonal=False):
        rows, offsets = [], []
        old = tops[j]
        new = old
        for origin, column in chunks:
            s = jnp.dot(k_all[origin, column], qt[j], preferred_element_type=jnp.float32)
            for b in range(PER):
                ks = swap[(origin * NX + (x if column == 0 else xk)) * PER + b]
                seen = (ks >= starts[j]) & (ks <= seqs[j])
                offset = jnp.where(seen, 0.0, MASKED).astype(jnp.float32)
                part = s[b * BLOCK:(b + 1) * BLOCK]
                if diagonal and b == j:
                    part = jnp.where(causal, part, MASKED)
                new = jnp.maximum(new, jnp.max(part, axis=0, keepdims=True) + offset)
                rows.append(part)
                offsets.append(offset)
        level = new * SCALE2
        weights = [
            jnp.exp2(part * SCALE2 - (level - offset)).astype(jnp.bfloat16) for part, offset in zip(rows, offsets)
        ]
        vals = jnp.concatenate([v_all[origin, column] for origin, column in chunks], axis=1)
        vals = jnp.concatenate([vals, jnp.ones((ONES, vals.shape[1]), jnp.bfloat16)], axis=0)
        product = jnp.dot(vals, jnp.concatenate(weights, axis=0), preferred_element_type=jnp.float32)
        acc[j] = acc[j] * jnp.exp2((old - new) * SCALE2) + product
        tops[j] = new

    def row(s, ways=(0, 1)):
        return [(zat(z - 1 - s) if w == 0 else zat(z + 1 + s), c) for w in ways for c in (0, 1)]

    def arrive(s, ways, onward):
        for stream in (0, 1, 2):
            for w in ways:
                zcopy(stream, w, s).wait_recv()
                if w in onward:
                    zcopy(stream, w, s + 1).start()
                if stream == 0:
                    vcopy(w * far + s, zat(z - 1 - s) if w == 0 else zat(z + 1 + s)).start()

    def mate_values(s, ways=(0, 1)):
        for w in ways:
            vcopy(w * far + s, z).wait_recv()

    own, other = range(PER), range(PER, 2 * PER)
    for j in own:
        absorb(j, [(z, 0)], diagonal=True)
    kmate.wait_recv()
    for w in (0, 1):
        zcopy(2, w, 0).start()
    arrive(0, (0, 1), (0, 1))
    vown.wait_recv()
    for j in own:
        absorb(j, [(z, 1)])
    arrive(1, (0, 1), (0, 1))
    mate_values(0)
    for j in own:
        absorb(j, row(0))
    for c in qmate:
        c.wait_recv()
    for j in other:
        absorb(j, [(z, 0), (z, 1)] + row(0))

    def step(s, _):
        arrive(s, (0, 1), (0, 1))
        mate_values(s - 1)
        for j in range(2 * PER):
            absorb(j, row(s - 1))
        return 0

    lax.fori_loop(2, far - 2, step, 0)
    arrive(far - 2, (0, 1), (0,))
    mate_values(far - 3)
    for j in range(2 * PER):
        absorb(j, row(far - 3))
    arrive(far - 1, (0,), ())
    mate_values(far - 2)
    for j in range(2 * PER):
        absorb(j, row(far - 2))
    mate_values(far - 1, (0,))

    ocopy = [remote(o_give.at[t], o_take.at[t], osend.at[t], orecv.at[t], query_mate) for t in range(PER)]
    scopy = [remote(s_give.at[t], s_take.at[t], ssend.at[t], srecv.at[t], query_mate) for t in range(PER)]
    for t in range(PER):
        j = PER + t
        absorb(j, row(far - 1, (0,)))
        total = acc[j, HD:HD + 1, :]
        some = total > 0.0
        total = jnp.where(some, total, 1.0)
        s_give[t] = jnp.where(some, tops[j] * SCALE2 + jnp.log2(total), MASKED)
        o_give[t] = (acc[j, :HD, :] / total).astype(jnp.bfloat16)
        scopy[t].start()
        ocopy[t].start()
    for j in own:
        absorb(j, row(far - 1, (0,)))

    def product(t, yy, cc):
        at = pl.multiple_of((yat(yy) * NC + cc) * cols, cols)
        return jnp.dot(
            att[t * BLOCK:(t + 1) * BLOCK, :], w_all[:, pl.ds(at, cols)], preferred_element_type=jnp.float32
        )

    order = hops + (0,)
    ccopy = [
        [remote(given.at[t, i], taken.at[t, i], csend.at[t, i], crecv.at[t, i], twin) for i in range(ny)]
        for t in range(PER)
    ]
    ycopy = [
        [
            remote(sums.at[t, i], finals.at[t, i], ysend.at[t, i], yrecv.at[t, i], ydev(y + d))
            for i, d in enumerate(hops)
        ]
        for t in range(PER)
    ]
    loads[3].wait()
    kept = []
    for t in range(PER):
        level = tops[t] * SCALE2
        total = acc[t, HD:HD + 1, :]
        scopy[t].wait_recv()
        ocopy[t].wait_recv()
        theirs = s_take[t]
        top = jnp.maximum(level + jnp.log2(total), theirs)
        mine = jnp.exp2(level - top)
        part = jnp.exp2(theirs - top)
        whole = mine * total + part
        mine, part = mine / whole, part / whole
        mixed = acc[t, :HD, :] * mine + o_take[t].astype(jnp.float32) * part
        for h in range(group):
            att[t * BLOCK:(t + 1) * BLOCK, h * HD:(h + 1) * HD] = (
                mixed[:, h * BLOCK:(h + 1) * BLOCK].T.astype(jnp.bfloat16)
            )
        for i, d in enumerate(order):
            given[t, i] = product(t, y + d, 1 - core).astype(jnp.bfloat16)
            ccopy[t][i].start()
        for i, d in enumerate(order):
            total = product(t, y + d, core)
            ccopy[t][i].wait_recv()
            total = total + taken[t, i].astype(jnp.float32)
            if d:
                sums[t, i] = total.astype(jnp.bfloat16)
                ycopy[t][i].start()
            else:
                kept.append(total)
    for t in range(PER):
        total = kept[t]
        for i in range(len(hops)):
            ycopy[t][i].wait_recv()
            total = total + finals[t, i].astype(jnp.float32)
        out_ref[t * BLOCK:(t + 1) * BLOCK, :] = total.astype(out_ref.dtype)

    kmate.wait_send()
    vown.wait_send()
    for c in qmate + ocopy + scopy + ccopy[0] + ccopy[1] + ycopy[0] + ycopy[1]:
        c.wait_send()

    def left(s, _):
        for stream in (0, 1, 2):
            for w in (0, 1):
                zcopy(stream, w, s).wait_send()
        for w in (0, 1):
            vcopy(w * far + s, z).wait_send()
        return 0

    lax.fori_loop(0, far - 1, left, 0)
    for stream in (0, 1, 2):
        zcopy(stream, 0, far - 1).wait_send()
    vcopy(far - 1, z).wait_send()


def local(queries, keys, values, out_weight, doc_blocks, swap_pairs, nz, ny):
    toks, feats = queries.shape
    dma = pltpu.SemaphoreType.DMA
    bf = jnp.bfloat16
    f32 = jnp.float32
    far = nz // 2
    cols = out_weight.shape[1] // (ny * NC)
    return pl.pallas_call(
        functools.partial(layer_kernel, nz, ny),
        out_shape=jax.ShapeDtypeStruct((toks, cols), bf),
        in_specs=[SMEM, SMEM, ANY, ANY, ANY, ANY],
        out_specs=VMEM,
        scratch_shapes=[
            pltpu.VMEM((toks, feats), bf),
            pltpu.VMEM((toks, HD), bf),
            pltpu.VMEM(out_weight.shape, bf),
            pltpu.VMEM((nz, 2, toks, HD), bf),
            pltpu.VMEM((nz, 2, HD, toks), bf),
            pltpu.VMEM((2 * PER, HD, feats), bf),
            pltpu.VMEM((2 * PER, HD + ONES, feats), f32),
            pltpu.VMEM((2 * PER, 1, feats), f32),
            pltpu.VMEM((PER, HD, feats), bf),
            pltpu.VMEM((PER, HD, feats), bf),
            pltpu.VMEM((PER, 1, feats), f32),
            pltpu.VMEM((PER, 1, feats), f32),
            pltpu.VMEM((toks, feats), bf),
            pltpu.VMEM((PER, ny, BLOCK, cols), bf),
            pltpu.VMEM((PER, ny, BLOCK, cols), bf),
            pltpu.VMEM((PER, ny - 1, BLOCK, cols), bf),
            pltpu.VMEM((PER, ny - 1, BLOCK, cols), bf),
            dma((4,)), dma((3, 2, far)), dma((3, 2, far)), dma((2 * far + 1,)), dma((2 * far + 1,)),
            dma, dma, dma((PER,)), dma((PER,)),
            dma((PER,)), dma((PER,)), dma((PER,)), dma((PER,)),
            dma((PER, ny)), dma((PER, ny)), dma((PER, ny - 1)), dma((PER, ny - 1)),
        ],
        compiler_params=pltpu.CompilerParams(
            collective_id=0, has_side_effects=True, vmem_limit_bytes=56 << 20
        ),
        name="layer",
    )(swap_pairs, doc_blocks, queries, keys, values, out_weight)


def solution(mesh):
    nz = mesh.shape["ctx"] // NX
    ny = mesh.shape["head"] // NC
    in_specs = (P("ctx", "head"), P("ctx", "head"), P("ctx", "head"), P("head", None), P(), P())
    return jax.shard_map(
        functools.partial(local, nz=nz, ny=ny),
        mesh=mesh, in_specs=in_specs, out_specs=P("ctx", "head"), check_vma=False,
    )
```

```python
import functools

import jax
import jax.numpy as jnp
from jax import lax
from jax.experimental import pallas as pl
from jax.experimental.pallas import tpu as pltpu
from jax.sharding import PartitionSpec as P

HD = 128
BLOCK = 128
NX = 4
NC = 2
PER = 2
ONES = 16
MIRROR = (0, 2, 1, 3)
SCALE2 = 1.4426950408889634 * HD ** (-0.5)
MASKED = -1e30
MESH = pl.DeviceIdType.MESH
ANY = pl.BlockSpec(memory_space=pl.ANY)
VMEM = pl.BlockSpec(memory_space=pltpu.VMEM)
SMEM = pl.BlockSpec(memory_space=pltpu.SMEM)


def layer_kernel(
    nz, ny,
    swap, docs, q_ref, k_ref, v_ref, w_ref, out_ref,
    q_in, v_in, w_all, k_all, v_all, qt, acc, tops,
    o_give, o_take, s_give, s_take, att, given, taken, sums, finals,
    lsem, zsend, zrecv, qsend, qrecv, osend, orecv, ssend, srecv, csend, crecv, ysend, yrecv,
):
    ctx = lax.axis_index("ctx")
    head = lax.axis_index("head")
    z, x = ctx // NX, lax.rem(ctx, NX)
    y, core = head // NC, lax.rem(head, NC)
    zat = lambda zz: lax.rem(zz + nz, nz)
    yat = lambda yy: lax.rem(yy + ny, ny)
    zdev = lambda d: (zat(z + d) * NX + x, head)
    columns = [x, lax.rem(x + 1, NX), lax.rem(x + NX - 1, NX), lax.rem(x + 2, NX)]
    peers = [(z * NX + c, head) for c in columns]
    twin = (ctx, y * NC + 1 - core)
    ydev = lambda yy: (ctx, yat(yy) * NC + core)
    hops = (2, 1, 3)
    stages = nz // 4
    group = qt.shape[2] // BLOCK
    cols = out_ref.shape[1]

    def remote(src, dst, send_sem, recv_sem, device):
        return pltpu.make_async_remote_copy(
            src_ref=src, dst_ref=dst, send_sem=send_sem, recv_sem=recv_sem, device_id=device, device_id_type=MESH
        )

    barrier = pltpu.get_barrier_semaphore()
    friends = [zdev(d) for d in (1, -1, 2, -2)] + peers[1:] + [twin] + [ydev(y + d) for d in hops]
    for device in friends:
        pl.semaphore_signal(barrier, inc=1, device_id=device, device_id_type=MESH)

    loads = [
        pltpu.make_async_copy(q_ref, q_in, lsem.at[0]),
        pltpu.make_async_copy(v_ref, v_in, lsem.at[1]),
        pltpu.make_async_copy(k_ref, k_all.at[z], lsem.at[2]),
        pltpu.make_async_copy(w_ref, w_all, lsem.at[3]),
    ]
    for c in loads:
        c.start()
    loads[1].wait()
    v_all[z] = v_in[...].T
    loads[0].wait()
    for t in range(PER):
        for h in range(group):
            qt[t, :, h * BLOCK:(h + 1) * BLOCK] = q_in[t * BLOCK:(t + 1) * BLOCK, h * HD:(h + 1) * HD].T
    loads[2].wait()
    pl.semaphore_wait(barrier, len(friends))

    def zcopy(stream, way, stage, leap):
        origin = zat(z - 2 * stage) if way == 0 else zat(z + 2 * stage)
        ref = (k_all if stream == 0 else v_all).at[origin]
        sems = (stream, way, stage, leap)
        return remote(ref, ref, zsend.at[sems], zrecv.at[sems], zdev((1 + leap) * (1 if way == 0 else -1)))

    def used(stream, way, stage, leap):
        return stage < stages - 1 or leap == 0 or stream == way

    zall = [
        (stream, way, stage, leap)
        for stage in range(stages) for leap in (1, 0) for stream in (0, 1) for way in (0, 1)
        if used(stream, way, stage, leap)
    ]
    zc = {key: zcopy(*key) for key in zall}
    pick = lambda stage, leap: [key for key in zall if key[2] == stage and key[3] == leap]
    qcopy = [
        [
            remote(qt.at[t], qt.at[PER * MIRROR[p] + t], qsend.at[p - 1, t], qrecv.at[MIRROR[p] - 1, t], peers[p])
            for t in range(PER)
        ]
        for p in range(1, NX)
    ]
    for key in pick(0, 1):
        zc[key].start()
    for p in range(1, NX):
        qcopy[p - 1][0].start()
    for key in pick(0, 0):
        zc[key].start()
    for p in range(1, NX):
        qcopy[p - 1][1].start()

    def arrive(stage):
        for key in pick(stage, 1):
            zc[key].wait_recv()
            onward = key[:2] + (stage + 1, 1)
            if onward in zc:
                zc[onward].start()
        if stage + 1 < stages:
            for key in pick(stage + 1, 0):
                zc[key].start()
        for key in pick(stage, 0):
            zc[key].wait_recv()

    def queries(p, t):
        qcopy[MIRROR[p] - 1][t].wait_recv()

    seqs, starts = [], []
    for j in range(NX * PER):
        seq = swap[(z * NX + columns[j // PER]) * PER + j % PER]
        start = jnp.int32(0)
        end = jnp.int32(0)
        for d in range(docs.shape[0]):
            end = end + docs[d]
            start = jnp.where(end <= seq, end, start)
        seqs.append(seq)
        starts.append(start)

    acc[...] = jnp.zeros_like(acc)
    tops[...] = jnp.full_like(tops, MASKED)
    wide = group * BLOCK
    causal = lax.broadcasted_iota(jnp.int32, (BLOCK, wide), 0) <= lax.rem(
        lax.broadcasted_iota(jnp.int32, (BLOCK, wide), 1), BLOCK
    )

    def absorb(j, chunks, diagonal=False):
        rows, offsets = [], []
        old = tops[j]
        new = old
        for origin in chunks:
            s = jnp.dot(k_all[origin], qt[j], preferred_element_type=jnp.float32)
            for b in range(PER):
                ks = swap[(origin * NX + x) * PER + b]
                seen = (ks >= starts[j]) & (ks <= seqs[j])
                offset = jnp.where(seen, 0.0, MASKED).astype(jnp.float32)
                part = s[b * BLOCK:(b + 1) * BLOCK]
                if diagonal and b == j:
                    part = jnp.where(causal, part, MASKED)
                new = jnp.maximum(new, jnp.max(part, axis=0, keepdims=True) + offset)
                rows.append(part)
                offsets.append(offset)
        level = new * SCALE2
        weights = [
            jnp.exp2(part * SCALE2 - (level - offset)).astype(jnp.bfloat16) for part, offset in zip(rows, offsets)
        ]
        vals = jnp.concatenate([v_all[origin] for origin in chunks], axis=1)
        vals = jnp.concatenate([vals, jnp.ones((ONES, vals.shape[1]), jnp.bfloat16)], axis=0)
        product = jnp.dot(vals, jnp.concatenate(weights, axis=0), preferred_element_type=jnp.float32)
        acc[j] = acc[j] * jnp.exp2((old - new) * SCALE2) + product
        tops[j] = new

    def batch(stage):
        near = [zat(z - 2 * stage - 1), zat(z + 2 * stage + 1), zat(z + 2 * stage + 2)]
        return near + ([zat(z - 2 * stage - 2)] if stage < stages - 1 else [])

    ocopy = [
        [
            remote(
                o_give.at[p - 1, t], o_take.at[MIRROR[p] - 1, t],
                osend.at[p - 1, t], orecv.at[MIRROR[p] - 1, t], peers[p],
            )
            for t in range(PER)
        ]
        for p in range(1, NX)
    ]
    scopy = [
        [
            remote(
                s_give.at[p - 1, t], s_take.at[MIRROR[p] - 1, t],
                ssend.at[p - 1, t], srecv.at[MIRROR[p] - 1, t], peers[p],
            )
            for t in range(PER)
        ]
        for p in range(1, NX)
    ]

    def give(p, t):
        j = PER * p + t
        total = acc[j, HD:HD + 1, :]
        some = total > 0.0
        total = jnp.where(some, total, 1.0)
        s_give[p - 1, t] = jnp.where(some, tops[j] * SCALE2 + jnp.log2(total), MASKED)
        o_give[p - 1, t] = (acc[j, :HD, :] / total).astype(jnp.bfloat16)
        scopy[p - 1][t].start()
        ocopy[p - 1][t].start()

    def product(t, yy, cc):
        at = pl.multiple_of((yat(yy) * NC + cc) * cols, cols)
        return jnp.dot(
            att[t * BLOCK:(t + 1) * BLOCK, :], w_all[:, pl.ds(at, cols)], preferred_element_type=jnp.float32
        )

    order = hops + (0,)
    ccopy = [
        [remote(given.at[t, i], taken.at[t, i], csend.at[t, i], crecv.at[t, i], twin) for i in range(ny)]
        for t in range(PER)
    ]
    ycopy = [
        [
            remote(sums.at[t, i], finals.at[t, i], ysend.at[t, i], yrecv.at[t, i], ydev(y + d))
            for i, d in enumerate(hops)
        ]
        for t in range(PER)
    ]

    def merge(t):
        for p in range(NX - 1):
            scopy[p][t].wait_recv()
            ocopy[p][t].wait_recv()
        levels = [tops[t] * SCALE2 + jnp.log2(acc[t, HD:HD + 1, :])] + [s_take[p, t] for p in range(NX - 1)]
        top = functools.reduce(jnp.maximum, levels)
        shares = [jnp.exp2(v - top) for v in levels]
        whole = functools.reduce(jnp.add, shares)
        mixed = acc[t, :HD, :] * (jnp.exp2(tops[t] * SCALE2 - top) / whole)
        for p in range(NX - 1):
            mixed = mixed + o_take[p, t].astype(jnp.float32) * (shares[p + 1] / whole)
        for h in range(group):
            att[t * BLOCK:(t + 1) * BLOCK, h * HD:(h + 1) * HD] = (
                mixed[:, h * BLOCK:(h + 1) * BLOCK].T.astype(jnp.bfloat16)
            )
        for i, d in enumerate(order):
            given[t, i] = product(t, y + d, 1 - core).astype(jnp.bfloat16)
            ccopy[t][i].start()

    def scatter(t):
        for i, d in enumerate(order):
            total = product(t, y + d, core)
            ccopy[t][i].wait_recv()
            total = total + taken[t, i].astype(jnp.float32)
            if d:
                sums[t, i] = total.astype(jnp.bfloat16)
                ycopy[t][i].start()
            else:
                return total

    def finish(t, total):
        for i in range(len(hops)):
            ycopy[t][i].wait_recv()
            total = total + finals[t, i].astype(jnp.float32)
        out_ref[t * BLOCK:(t + 1) * BLOCK, :] = total.astype(out_ref.dtype)

    own = (0, 1)
    for j in own:
        absorb(j, [z], diagonal=True)
    arrive(0)
    for j in own:
        absorb(j, batch(0))
    for p in (1, 2):
        queries(p, 0)
        absorb(PER * p, [z] + batch(0))
    arrive(1)
    queries(3, 0)
    absorb(PER * 3, [z] + batch(0))
    for p in range(NX):
        absorb(PER * p, batch(1))
    arrive(2)
    for p in range(NX):
        absorb(PER * p, batch(2))
    arrive(3)
    for p in (3, 1, 2):
        absorb(PER * p, batch(3))
        give(p, 0)
    absorb(0, batch(3))
    loads[3].wait()
    for p in (3, 1, 2):
        queries(p, 1)
        absorb(PER * p + 1, [z] + batch(0) + batch(3))
        absorb(PER * p + 1, batch(1) + batch(2))
        give(p, 1)
        if p == 1:
            merge(0)
    first = scatter(0)
    absorb(1, batch(1) + batch(2) + batch(3))
    merge(1)
    second = scatter(1)
    finish(0, first)
    finish(1, second)

    for copies in qcopy + ocopy + scopy + ccopy + ycopy:
        for c in copies:
            c.wait_send()
    for key in zall:
        zc[key].wait_send()


def local(queries, keys, values, out_weight, doc_blocks, swap_pairs, nz, ny):
    toks, feats = queries.shape
    dma = pltpu.SemaphoreType.DMA
    bf = jnp.bfloat16
    f32 = jnp.float32
    cols = out_weight.shape[1] // (ny * NC)
    return pl.pallas_call(
        functools.partial(layer_kernel, nz, ny),
        out_shape=jax.ShapeDtypeStruct((toks, cols), bf),
        in_specs=[SMEM, SMEM, ANY, ANY, ANY, ANY],
        out_specs=VMEM,
        scratch_shapes=[
            pltpu.VMEM((toks, feats), bf),
            pltpu.VMEM((toks, HD), bf),
            pltpu.VMEM(out_weight.shape, bf),
            pltpu.VMEM((nz, toks, HD), bf),
            pltpu.VMEM((nz, HD, toks), bf),
            pltpu.VMEM((NX * PER, HD, feats), bf),
            pltpu.VMEM((NX * PER, HD + ONES, feats), f32),
            pltpu.VMEM((NX * PER, 1, feats), f32),
            pltpu.VMEM((NX - 1, PER, HD, feats), bf),
            pltpu.VMEM((NX - 1, PER, HD, feats), bf),
            pltpu.VMEM((NX - 1, PER, 1, feats), f32),
            pltpu.VMEM((NX - 1, PER, 1, feats), f32),
            pltpu.VMEM((toks, feats), bf),
            pltpu.VMEM((PER, ny, BLOCK, cols), bf),
            pltpu.VMEM((PER, ny, BLOCK, cols), bf),
            pltpu.VMEM((PER, ny - 1, BLOCK, cols), bf),
            pltpu.VMEM((PER, ny - 1, BLOCK, cols), bf),
            dma((4,)), dma((2, 2, nz // 4, 2)), dma((2, 2, nz // 4, 2)),
            dma((NX - 1, PER)), dma((NX - 1, PER)), dma((NX - 1, PER)), dma((NX - 1, PER)),
            dma((NX - 1, PER)), dma((NX - 1, PER)),
            dma((PER, ny)), dma((PER, ny)), dma((PER, ny - 1)), dma((PER, ny - 1)),
        ],
        compiler_params=pltpu.CompilerParams(
            collective_id=0, has_side_effects=True, vmem_limit_bytes=56 << 20
        ),
        name="layer",
    )(swap_pairs, doc_blocks, queries, keys, values, out_weight)


def solution(mesh):
    nz = mesh.shape["ctx"] // NX
    ny = mesh.shape["head"] // NC
    in_specs = (P("ctx", "head"), P("ctx", "head"), P("ctx", "head"), P("head", None), P(), P())
    return jax.shard_map(
        functools.partial(local, nz=nz, ny=ny),
        mesh=mesh, in_specs=in_specs, out_specs=P("ctx", "head"), check_vma=False,
    )
```

```python
import functools

import jax
import jax.numpy as jnp
from jax import lax
from jax.experimental import pallas as pl
from jax.experimental.pallas import tpu as pltpu
from jax.sharding import PartitionSpec as P

HD = 128
BLOCK = 128
NX = 4
NC = 2
PER = 2
ONES = 16
SPLIT = 2
PARTS = 2
SUB = BLOCK // PARTS
MIRROR = (0, 2, 1, 3)
SCALE2 = 1.4426950408889634 * HD ** (-0.5)
MASKED = -1e30
MESH = pl.DeviceIdType.MESH
ANY = pl.BlockSpec(memory_space=pl.ANY)
VMEM = pl.BlockSpec(memory_space=pltpu.VMEM)
SMEM = pl.BlockSpec(memory_space=pltpu.SMEM)


def layer_kernel(
    nz, ny,
    swap, docs, q_ref, k_ref, v_ref, w_ref, out_ref,
    q_in, v_in, w_all, k_all, v_all, qt, acc, tops,
    o_give, o_take, s_give, s_take, att, given, taken, sums, finals, kept,
    lsem, zsend, zrecv, qsend, qrecv, osend, orecv, ssend, srecv, csend, crecv, ysend, yrecv,
):
    ctx = lax.axis_index("ctx")
    head = lax.axis_index("head")
    z, x = ctx // NX, lax.rem(ctx, NX)
    y, core = head // NC, lax.rem(head, NC)
    zat = lambda zz: lax.rem(zz + nz, nz)
    yat = lambda yy: lax.rem(yy + ny, ny)
    zdev = lambda d: (zat(z + d) * NX + x, head)
    columns = [x, lax.rem(x + 1, NX), lax.rem(x + NX - 1, NX), lax.rem(x + 2, NX)]
    peers = [(z * NX + c, head) for c in columns]
    twin = (ctx, y * NC + 1 - core)
    ydev = lambda yy: (ctx, yat(yy) * NC + core)
    hops = (2, 1, 3)
    far = nz // 2
    group = qt.shape[2] // BLOCK
    cols = out_ref.shape[1]

    def remote(src, dst, send_sem, recv_sem, device):
        return pltpu.make_async_remote_copy(
            src_ref=src, dst_ref=dst, send_sem=send_sem, recv_sem=recv_sem, device_id=device, device_id_type=MESH
        )

    barrier = pltpu.get_barrier_semaphore()
    friends = [zdev(d) for d in (1, -1)] + peers[1:] + [twin] + [ydev(y + d) for d in hops]
    for device in friends:
        pl.semaphore_signal(barrier, inc=1, device_id=device, device_id_type=MESH)

    loads = [
        pltpu.make_async_copy(q_ref, q_in, lsem.at[0]),
        pltpu.make_async_copy(v_ref, v_in, lsem.at[1]),
        pltpu.make_async_copy(k_ref, k_all.at[z], lsem.at[2]),
        pltpu.make_async_copy(w_ref, w_all, lsem.at[3]),
    ]
    for c in loads:
        c.start()
    loads[1].wait()
    v_all[z] = v_in[...].T
    loads[0].wait()
    for t in range(PER):
        for h in range(group):
            turned = q_in[t * BLOCK:(t + 1) * BLOCK, h * HD:(h + 1) * HD].T
            for u in range(PARTS):
                qt[t, :, (u * group + h) * SUB:(u * group + h + 1) * SUB] = turned[:, u * SUB:(u + 1) * SUB]
    loads[2].wait()
    pl.semaphore_wait(barrier, len(friends))

    def zcopy(stream, way, step):
        origin = zat(z - step) if way == 0 else zat(z + step)
        ref = k_all if stream < SPLIT else v_all
        size = ref.shape[1] // SPLIT
        ref = ref.at[origin, pl.ds(stream % SPLIT * size, size)]
        sems = (stream, way, step)
        return remote(ref, ref, zsend.at[sems], zrecv.at[sems], zdev(1 if way == 0 else -1))

    zall = [
        (stream, way, step)
        for step in range(far) for stream in range(2 * SPLIT) for way in (0, 1)
        if step < far - 1 or (stream < SPLIT) == (way == 0)
    ]
    zc = {key: zcopy(*key) for key in zall}
    pick = lambda step: [key for key in zall if key[2] == step]
    qcopy = [
        [
            remote(qt.at[t], qt.at[PER * MIRROR[p] + t], qsend.at[p - 1, t], qrecv.at[MIRROR[p] - 1, t], peers[p])
            for t in range(PER)
        ]
        for p in range(1, NX)
    ]
    for key in pick(0):
        zc[key].start()
    for p in (1, 2, 3):
        qcopy[p - 1][0].start()

    def arrive(step, streams=range(2 * SPLIT)):
        for key in pick(step):
            if key[0] not in streams:
                continue
            zc[key].wait_recv()
            onward = key[:2] + (step + 1,)
            if onward in zc:
                zc[onward].start()

    def queries(p, t):
        qcopy[MIRROR[p] - 1][t].wait_recv()

    seqs, starts = [], []
    for j in range(NX * PER):
        seq = swap[(z * NX + columns[j // PER]) * PER + j % PER]
        start = jnp.int32(0)
        end = jnp.int32(0)
        for d in range(docs.shape[0]):
            end = end + docs[d]
            start = jnp.where(end <= seq, end, start)
        seqs.append(seq)
        starts.append(start)

    acc[...] = jnp.zeros_like(acc)
    tops[...] = jnp.full_like(tops, MASKED)
    wide = group * SUB
    lane = lax.broadcasted_iota(jnp.int32, (BLOCK, PARTS * wide), 1)
    causal = lax.broadcasted_iota(jnp.int32, (BLOCK, PARTS * wide), 0) <= lane // wide * SUB + lax.rem(lane, SUB)

    def score(j, chunks, diagonal=False):
        rows, offsets = [], []
        new = tops[j]
        for origin in chunks:
            s = jnp.dot(k_all[origin], qt[j], preferred_element_type=jnp.float32)
            for b in range(PER):
                ks = swap[(origin * NX + x) * PER + b]
                seen = (ks >= starts[j]) & (ks <= seqs[j])
                offset = jnp.where(seen, 0.0, MASKED).astype(jnp.float32)
                part = s[b * BLOCK:(b + 1) * BLOCK]
                if diagonal and b == j:
                    part = jnp.where(causal, part, MASKED)
                new = jnp.maximum(new, jnp.max(part, axis=0, keepdims=True) + offset)
                rows.append(part)
                offsets.append(offset)
        return j, chunks, rows, offsets, new

    def absorb(j, chunks, rows, offsets, new):
        level = new * SCALE2
        weights = [
            jnp.exp2(part * SCALE2 - (level - offset)).astype(jnp.bfloat16) for part, offset in zip(rows, offsets)
        ]
        vals = jnp.concatenate([v_all[origin] for origin in chunks], axis=1)
        vals = jnp.concatenate([vals, jnp.ones((ONES, vals.shape[1]), jnp.bfloat16)], axis=0)
        product = jnp.dot(vals, jnp.concatenate(weights, axis=0), preferred_element_type=jnp.float32)
        acc[j] = acc[j] * jnp.exp2((tops[j] - new) * SCALE2) + product
        tops[j] = new

    def attend(units, done=lambda p, t: None):
        ask = lambda p, t, rows: score(PER * p + t, [c for r in rows for c in row(r)])
        asked = ask(*units[0])
        for n, (p, t, _) in enumerate(units):
            ahead = ask(*units[n + 1]) if n + 1 < len(units) else None
            absorb(*asked)
            done(p, t)
            asked = ahead

    def row(step):
        if step < 0:
            return [z]
        return [zat(z - 1 - step), zat(z + 1 + step)] if step < far - 1 else [zat(z + far)]

    pieces = [(t, u) for t in range(PER) for u in range(PARTS)]

    def back(give_ref, take_ref, sends, recvs, p, i):
        m = MIRROR[p] - 1
        return remote(
            give_ref.at[p - 1, i], take_ref.at[m, i], sends.at[p - 1, i], recvs.at[m, i], peers[p]
        )

    ocopy = [[back(o_give, o_take, osend, orecv, p, i) for i in range(len(pieces))] for p in range(1, NX)]
    scopy = [[back(s_give, s_take, ssend, srecv, p, i) for i in range(len(pieces))] for p in range(1, NX)]

    def give(p, i):
        t, u = pieces[i]
        j = PER * p + t
        lanes = slice(u * wide, (u + 1) * wide)
        total = acc[j, HD:HD + 1, lanes]
        some = total > 0.0
        total = jnp.where(some, total, 1.0)
        s_give[p - 1, i] = jnp.where(some, tops[j, :, lanes] * SCALE2 + jnp.log2(total), MASKED)
        o_give[p - 1, i] = (acc[j, :HD, lanes] / total).astype(jnp.bfloat16)
        scopy[p - 1][i].start()
        ocopy[p - 1][i].start()

    def product(i, yy, cc):
        at = pl.multiple_of((yat(yy) * NC + cc) * cols, cols)
        return jnp.dot(att[i * SUB:(i + 1) * SUB, :], w_all[:, pl.ds(at, cols)], preferred_element_type=jnp.float32)

    order = hops + (0,)
    ccopy = [
        [remote(given.at[i, n], taken.at[i, n], csend.at[i, n], crecv.at[i, n], twin) for n in range(ny)]
        for i in range(len(pieces))
    ]
    ycopy = [
        [
            remote(sums.at[i, n], finals.at[i, n], ysend.at[i, n], yrecv.at[i, n], ydev(y + d))
            for n, d in enumerate(hops)
        ]
        for i in range(len(pieces))
    ]

    def merge(i):
        t, u = pieces[i]
        lanes = slice(u * wide, (u + 1) * wide)
        for p in range(NX - 1):
            scopy[p][i].wait_recv()
            ocopy[p][i].wait_recv()
        own_level = tops[t, :, lanes] * SCALE2
        levels = [own_level + jnp.log2(acc[t, HD:HD + 1, lanes])] + [s_take[p, i] for p in range(NX - 1)]
        top = functools.reduce(jnp.maximum, levels)
        shares = [jnp.exp2(v - top) for v in levels]
        whole = functools.reduce(jnp.add, shares)
        mixed = acc[t, :HD, lanes] * (jnp.exp2(own_level - top) / whole)
        for p in range(NX - 1):
            mixed = mixed + o_take[p, i].astype(jnp.float32) * (shares[p + 1] / whole)
        for h in range(group):
            att[i * SUB:(i + 1) * SUB, h * HD:(h + 1) * HD] = (
                mixed[:, h * SUB:(h + 1) * SUB].T.astype(jnp.bfloat16)
            )
        for n, d in enumerate(order):
            given[i, n] = product(i, y + d, 1 - core).astype(jnp.bfloat16)
            ccopy[i][n].start()

    def scatter(i):
        for n, d in enumerate(order):
            total = product(i, y + d, core)
            ccopy[i][n].wait_recv()
            total = total + taken[i, n].astype(jnp.float32)
            if d:
                sums[i, n] = total.astype(jnp.bfloat16)
                ycopy[i][n].start()
            else:
                kept[i] = total

    def finish(i):
        total = kept[i]
        for n in range(len(hops)):
            ycopy[i][n].wait_recv()
            total = total + finals[i, n].astype(jnp.float32)
        out_ref[i * SUB:(i + 1) * SUB, :] = total.astype(out_ref.dtype)

    last = far - 1
    table = [
        [(0, 0, [0]), (0, 1, [0])],
        [(1, 0, [-1, 0, 1]), (2, 0, [-1, 0, 1]), (0, 0, [1])],
        [(3, 0, [-1, 0, 1, 2]), (1, 1, [-1, 0, 1, 2]), (2, 1, [-1, 0, 1, 2])],
        [(3, 1, [-1, 0, 1, 2, 3]), (0, 0, [2, 3]), (0, 1, [1, 2, 3])],
        [(1, 0, [2, 3, 4]), (2, 0, [2, 3, 4]), (3, 0, [3, 4])],
        [(1, 1, [3, 4, 5]), (2, 1, [3, 4, 5]), (3, 1, [4, 5])],
        [(3, 0, [5, 6]), (1, 0, [5, 6]), (2, 0, [5, 6]), (0, 0, [4, 5, 6])],
    ]
    for t in range(PER):
        absorb(*score(t, [z], diagonal=True))

    def second_half(p):
        qcopy[p - 1][0].wait_send()
        qcopy[p - 1][1].start()

    second_half(1)
    second_half(2)
    asked = set()
    for step, units in enumerate(table):
        arrive(step)
        if step == 0:
            second_half(3)
        for p, t, _ in units:
            if p and (p, t) not in asked:
                queries(p, t)
                asked.add((p, t))
        attend(units)
    arrive(last)

    def done(p, t):
        for u in range(PARTS if t == 0 else 1):
            if p:
                give(p, PARTS * t + u)

    ends = [(p, 0, [last]) for p in (3, 1, 2, 0)] + [(p, 1, [last - 1, last]) for p in (3, 1, 2)]
    attend(ends + [(0, 1, [last - 3, last - 2, last - 1, last])], done)
    for p in (3, 1, 2):
        for u in range(1, PARTS):
            give(p, PARTS + u)
    loads[3].wait()
    for i in range(len(pieces)):
        merge(i)
        if i:
            scatter(i - 1)
    scatter(len(pieces) - 1)
    for i in range(len(pieces)):
        finish(i)

    for c in [copies[1] for copies in qcopy]:
        c.wait_send()
    for copies in ocopy + scopy + ccopy + ycopy:
        for c in copies:
            c.wait_send()
    for key in zall:
        zc[key].wait_send()


def local(queries, keys, values, out_weight, doc_blocks, swap_pairs, nz, ny):
    toks, feats = queries.shape
    dma = pltpu.SemaphoreType.DMA
    bf = jnp.bfloat16
    f32 = jnp.float32
    cols = out_weight.shape[1] // (ny * NC)
    parts = PER * PARTS
    return pl.pallas_call(
        functools.partial(layer_kernel, nz, ny),
        out_shape=jax.ShapeDtypeStruct((toks, cols), bf),
        in_specs=[SMEM, SMEM, ANY, ANY, ANY, ANY],
        out_specs=VMEM,
        scratch_shapes=[
            pltpu.VMEM((toks, feats), bf),
            pltpu.VMEM((toks, HD), bf),
            pltpu.VMEM(out_weight.shape, bf),
            pltpu.VMEM((nz, toks, HD), bf),
            pltpu.VMEM((nz, HD, toks), bf),
            pltpu.VMEM((NX * PER, HD, feats), bf),
            pltpu.VMEM((NX * PER, HD + ONES, feats), f32),
            pltpu.VMEM((NX * PER, 1, feats), f32),
            pltpu.VMEM((NX - 1, parts, HD, feats // PARTS), bf),
            pltpu.VMEM((NX - 1, parts, HD, feats // PARTS), bf),
            pltpu.VMEM((NX - 1, parts, 1, feats // PARTS), f32),
            pltpu.VMEM((NX - 1, parts, 1, feats // PARTS), f32),
            pltpu.VMEM((toks, feats), bf),
            pltpu.VMEM((parts, ny, SUB, cols), bf),
            pltpu.VMEM((parts, ny, SUB, cols), bf),
            pltpu.VMEM((parts, ny - 1, SUB, cols), bf),
            pltpu.VMEM((parts, ny - 1, SUB, cols), bf),
            pltpu.VMEM((parts, SUB, cols), f32),
            dma((4,)), dma((2 * SPLIT, 2, nz // 2)), dma((2 * SPLIT, 2, nz // 2)),
            dma((NX - 1, PER)), dma((NX - 1, PER)),
            dma((NX - 1, parts)), dma((NX - 1, parts)), dma((NX - 1, parts)), dma((NX - 1, parts)),
            dma((parts, ny)), dma((parts, ny)), dma((parts, ny - 1)), dma((parts, ny - 1)),
        ],
        compiler_params=pltpu.CompilerParams(
            collective_id=0, has_side_effects=True, vmem_limit_bytes=56 << 20
        ),
        name="layer",
    )(swap_pairs, doc_blocks, queries, keys, values, out_weight)


def solution(mesh):
    nz = mesh.shape["ctx"] // NX
    ny = mesh.shape["head"] // NC
    in_specs = (P("ctx", "head"), P("ctx", "head"), P("ctx", "head"), P("head", None), P(), P())
    return jax.shard_map(
        functools.partial(local, nz=nz, ny=ny),
        mesh=mesh, in_specs=in_specs, out_specs=P("ctx", "head"), check_vma=False,
    )
```

```python
import functools

import jax
import jax.numpy as jnp
from jax import lax
from jax.experimental import pallas as pl
from jax.experimental.pallas import tpu as pltpu
from jax.sharding import PartitionSpec as P

HD = 128
BLOCK = 128
NX = 4
NC = 2
PER = 2
ONES = 16
SPLIT = 2
PARTS = 2
SUB = BLOCK // PARTS
MIRROR = (0, 2, 1, 3)
SCALE2 = 1.4426950408889634 * HD ** (-0.5)
MASKED = -1e30
MESH = pl.DeviceIdType.MESH
ANY = pl.BlockSpec(memory_space=pl.ANY)
VMEM = pl.BlockSpec(memory_space=pltpu.VMEM)
SMEM = pl.BlockSpec(memory_space=pltpu.SMEM)


def layer_kernel(
    nz, ny,
    swap, docs, q_ref, k_ref, v_ref, w_ref, out_ref,
    q_in, v_in, w_all, k_all, v_all, qt, acc, tops,
    o_give, o_take, s_give, s_take, att, given, taken, sums, finals, kept,
    lsem, zsend, zrecv, qsend, qrecv, osend, orecv, ssend, srecv, csend, crecv, ysend, yrecv,
):
    ctx = lax.axis_index("ctx")
    head = lax.axis_index("head")
    z, x = ctx // NX, lax.rem(ctx, NX)
    y, core = head // NC, lax.rem(head, NC)
    zat = lambda zz: lax.rem(zz + nz, nz)
    yat = lambda yy: lax.rem(yy + ny, ny)
    zdev = lambda d: (zat(z + d) * NX + x, head)
    columns = [x, lax.rem(x + 1, NX), lax.rem(x + NX - 1, NX), lax.rem(x + 2, NX)]
    peers = [(z * NX + c, head) for c in columns]
    twin = (ctx, y * NC + 1 - core)
    ydev = lambda yy: (ctx, yat(yy) * NC + core)
    hops = (2, 1, 3)
    far = nz // 2
    group = qt.shape[2] // BLOCK
    cols = out_ref.shape[1]

    def remote(src, dst, send_sem, recv_sem, device):
        return pltpu.make_async_remote_copy(
            src_ref=src, dst_ref=dst, send_sem=send_sem, recv_sem=recv_sem, device_id=device, device_id_type=MESH
        )

    barrier = pltpu.get_barrier_semaphore()
    friends = [zdev(d) for d in (1, -1)] + peers[1:] + [twin] + [ydev(y + d) for d in hops]
    for device in friends:
        pl.semaphore_signal(barrier, inc=1, device_id=device, device_id_type=MESH)

    loads = [
        pltpu.make_async_copy(q_ref, q_in, lsem.at[0]),
        pltpu.make_async_copy(v_ref, v_in, lsem.at[1]),
        pltpu.make_async_copy(k_ref, k_all.at[z], lsem.at[2]),
        pltpu.make_async_copy(w_ref, w_all, lsem.at[3]),
    ]
    for c in loads:
        c.start()
    loads[1].wait()
    v_all[z] = v_in[...].T
    loads[0].wait()
    for t in range(PER):
        for h in range(group):
            turned = q_in[t * BLOCK:(t + 1) * BLOCK, h * HD:(h + 1) * HD].T
            for u in range(PARTS):
                qt[t, :, (u * group + h) * SUB:(u * group + h + 1) * SUB] = turned[:, u * SUB:(u + 1) * SUB]
    loads[2].wait()
    pl.semaphore_wait(barrier, len(friends))

    def zcopy(stream, way, step):
        origin = zat(z - step) if way == 0 else zat(z + step)
        ref = k_all if stream < SPLIT else v_all
        size = ref.shape[1] // SPLIT
        ref = ref.at[origin, pl.ds(stream % SPLIT * size, size)]
        sems = (stream, way, step)
        return remote(ref, ref, zsend.at[sems], zrecv.at[sems], zdev(1 if way == 0 else -1))

    zall = [
        (stream, way, step)
        for step in range(far) for stream in range(2 * SPLIT) for way in (0, 1)
        if step < far - 1 or (stream < SPLIT) == (way == 0)
    ]
    zc = {key: zcopy(*key) for key in zall}
    pick = lambda step: [key for key in zall if key[2] == step]
    qcopy = [
        [
            remote(qt.at[t], qt.at[PER * MIRROR[p] + t], qsend.at[p - 1, t], qrecv.at[MIRROR[p] - 1, t], peers[p])
            for t in range(PER)
        ]
        for p in range(1, NX)
    ]
    for key in pick(0):
        zc[key].start()
    for p in (1, 2, 3):
        qcopy[p - 1][0].start()

    def arrive(step, streams=range(2 * SPLIT)):
        for key in pick(step):
            if key[0] not in streams:
                continue
            zc[key].wait_recv()
            onward = key[:2] + (step + 1,)
            if onward in zc:
                zc[onward].start()

    def queries(p, t):
        qcopy[MIRROR[p] - 1][t].wait_recv()

    seqs, starts = [], []
    for j in range(NX * PER):
        seq = swap[(z * NX + columns[j // PER]) * PER + j % PER]
        start = jnp.int32(0)
        end = jnp.int32(0)
        for d in range(docs.shape[0]):
            end = end + docs[d]
            start = jnp.where(end <= seq, end, start)
        seqs.append(seq)
        starts.append(start)

    acc[...] = jnp.zeros_like(acc)
    tops[...] = jnp.full_like(tops, MASKED)
    wide = group * SUB
    lane = lax.broadcasted_iota(jnp.int32, (BLOCK, PARTS * wide), 1)
    causal = lax.broadcasted_iota(jnp.int32, (BLOCK, PARTS * wide), 0) <= lane // wide * SUB + lax.rem(lane, SUB)

    def score(j, chunks, diagonal=False):
        rows, offsets = [], []
        new = tops[j]
        for origin in chunks:
            s = jnp.dot(k_all[origin], qt[j], preferred_element_type=jnp.float32)
            for b in range(PER):
                ks = swap[(origin * NX + x) * PER + b]
                seen = (ks >= starts[j]) & (ks <= seqs[j])
                offset = jnp.where(seen, 0.0, MASKED).astype(jnp.float32)
                part = s[b * BLOCK:(b + 1) * BLOCK]
                if diagonal and b == j:
                    part = jnp.where(causal, part, MASKED)
                new = jnp.maximum(new, jnp.max(part, axis=0, keepdims=True) + offset)
                rows.append(part)
                offsets.append(offset)
        return j, chunks, rows, offsets, new

    def absorb(j, chunks, rows, offsets, new):
        level = new * SCALE2
        weights = [
            jnp.exp2(part * SCALE2 - (level - offset)).astype(jnp.bfloat16) for part, offset in zip(rows, offsets)
        ]
        vals = jnp.concatenate([v_all[origin] for origin in chunks], axis=1)
        vals = jnp.concatenate([vals, jnp.ones((ONES, vals.shape[1]), jnp.bfloat16)], axis=0)
        product = jnp.dot(vals, jnp.concatenate(weights, axis=0), preferred_element_type=jnp.float32)
        acc[j] = acc[j] * jnp.exp2((tops[j] - new) * SCALE2) + product
        tops[j] = new

    def attend(units, done=lambda p, t: None):
        ask = lambda p, t, rows: score(PER * p + t, [c for r in rows for c in row(r)])
        asked = ask(*units[0])
        for n, (p, t, _) in enumerate(units):
            more = units[n + 1:n + 2]
            early = [u for u in more if u[:2] != (p, t)]
            ahead = ask(*early[0]) if early else None
            absorb(*asked)
            done(p, t)
            asked = ask(*more[0]) if more and not early else ahead

    def row(step):
        if step < 0:
            return [z]
        return [zat(z - 1 - step), zat(z + 1 + step)] if step < far - 1 else [zat(z + far)]

    pieces = [(t, u) for t in range(PER) for u in range(PARTS)]

    def back(give_ref, take_ref, sends, recvs, p, i):
        m = MIRROR[p] - 1
        return remote(
            give_ref.at[p - 1, i], take_ref.at[m, i], sends.at[p - 1, i], recvs.at[m, i], peers[p]
        )

    ocopy = [[back(o_give, o_take, osend, orecv, p, i) for i in range(len(pieces))] for p in range(1, NX)]
    scopy = [[back(s_give, s_take, ssend, srecv, p, i) for i in range(len(pieces))] for p in range(1, NX)]

    def give(p, i):
        t, u = pieces[i]
        j = PER * p + t
        lanes = slice(u * wide, (u + 1) * wide)
        total = acc[j, HD:HD + 1, lanes]
        some = total > 0.0
        total = jnp.where(some, total, 1.0)
        s_give[p - 1, i] = jnp.where(some, tops[j, :, lanes] * SCALE2 + jnp.log2(total), MASKED)
        o_give[p - 1, i] = (acc[j, :HD, lanes] / total).astype(jnp.bfloat16)
        scopy[p - 1][i].start()
        ocopy[p - 1][i].start()

    def product(i, yy, cc):
        at = pl.multiple_of((yat(yy) * NC + cc) * cols, cols)
        return jnp.dot(att[i * SUB:(i + 1) * SUB, :], w_all[:, pl.ds(at, cols)], preferred_element_type=jnp.float32)

    order = hops + (0,)
    ccopy = [
        [remote(given.at[i, n], taken.at[i, n], csend.at[i, n], crecv.at[i, n], twin) for n in range(ny)]
        for i in range(len(pieces))
    ]
    ycopy = [
        [
            remote(sums.at[i, n], finals.at[i, n], ysend.at[i, n], yrecv.at[i, n], ydev(y + d))
            for n, d in enumerate(hops)
        ]
        for i in range(len(pieces))
    ]

    def merge(i):
        t, u = pieces[i]
        lanes = slice(u * wide, (u + 1) * wide)
        for p in range(NX - 1):
            scopy[p][i].wait_recv()
            ocopy[p][i].wait_recv()
        own_level = tops[t, :, lanes] * SCALE2
        levels = [own_level + jnp.log2(acc[t, HD:HD + 1, lanes])] + [s_take[p, i] for p in range(NX - 1)]
        top = functools.reduce(jnp.maximum, levels)
        shares = [jnp.exp2(v - top) for v in levels]
        whole = functools.reduce(jnp.add, shares)
        mixed = acc[t, :HD, lanes] * (jnp.exp2(own_level - top) / whole)
        for p in range(NX - 1):
            mixed = mixed + o_take[p, i].astype(jnp.float32) * (shares[p + 1] / whole)
        for h in range(group):
            att[i * SUB:(i + 1) * SUB, h * HD:(h + 1) * HD] = (
                mixed[:, h * SUB:(h + 1) * SUB].T.astype(jnp.bfloat16)
            )
        for n, d in enumerate(order):
            given[i, n] = product(i, y + d, 1 - core).astype(jnp.bfloat16)
            ccopy[i][n].start()

    def scatter(i):
        for n, d in enumerate(order):
            total = product(i, y + d, core)
            ccopy[i][n].wait_recv()
            total = total + taken[i, n].astype(jnp.float32)
            if d:
                sums[i, n] = total.astype(jnp.bfloat16)
                ycopy[i][n].start()
            else:
                kept[i] = total

    def finish(i):
        total = kept[i]
        for n in range(len(hops)):
            ycopy[i][n].wait_recv()
            total = total + finals[i, n].astype(jnp.float32)
        out_ref[i * SUB:(i + 1) * SUB, :] = total.astype(out_ref.dtype)

    last = far - 1
    table = [
        [(0, 0, [0]), (0, 1, [0])],
        [(1, 0, [-1, 0, 1]), (2, 0, [-1, 0, 1]), (0, 0, [1])],
        [(3, 0, [-1, 0, 1, 2]), (1, 1, [-1, 0, 1, 2]), (2, 1, [-1, 0, 1, 2])],
        [(3, 1, [-1, 0, 1, 2, 3])],
        [(1, 0, [2, 3, 4]), (2, 0, [2, 3, 4]), (3, 0, [3, 4])],
        [(1, 1, [3, 4, 5]), (2, 1, [3, 4, 5]), (3, 1, [4, 5])],
        [(3, 0, [5, 6]), (1, 0, [5, 6]), (2, 0, [5, 6])],
    ]
    for t in range(PER):
        absorb(*score(t, [z], diagonal=True))

    def second_half(p):
        qcopy[p - 1][0].wait_send()
        qcopy[p - 1][1].start()

    second_half(1)
    second_half(2)
    asked = set()
    for step, units in enumerate(table):
        arrive(step)
        if step == 0:
            second_half(3)
        for p, t, _ in units:
            if p and (p, t) not in asked:
                queries(p, t)
                asked.add((p, t))
        attend(units)
    arrive(last)

    def done(p, t):
        if p and t == 0:
            for u in range(PARTS):
                give(p, u)
        elif p:
            give(p, PARTS)
        if (p, t) == (2, 1):
            for u in range(1, PARTS):
                for peer in (3, 1, 2):
                    give(peer, PARTS + u)

    ends = [(p, 0, [last]) for p in (3, 1, 2)] + [(p, 1, [last - 1, last]) for p in (3, 1, 2)]
    ends += [(0, 0, [2, 3, 4]), (0, 1, [1, 2, 3, 4]), (0, 0, [5, 6, last]), (0, 1, [5, 6, last])]
    attend(ends, done)
    loads[3].wait()
    for i in range(len(pieces)):
        merge(i)
        if i:
            scatter(i - 1)
    scatter(len(pieces) - 1)
    for i in range(len(pieces)):
        finish(i)

    for c in [copies[1] for copies in qcopy]:
        c.wait_send()
    for copies in ocopy + scopy + ccopy + ycopy:
        for c in copies:
            c.wait_send()
    for key in zall:
        zc[key].wait_send()


def local(queries, keys, values, out_weight, doc_blocks, swap_pairs, nz, ny):
    toks, feats = queries.shape
    dma = pltpu.SemaphoreType.DMA
    bf = jnp.bfloat16
    f32 = jnp.float32
    cols = out_weight.shape[1] // (ny * NC)
    parts = PER * PARTS
    return pl.pallas_call(
        functools.partial(layer_kernel, nz, ny),
        out_shape=jax.ShapeDtypeStruct((toks, cols), bf),
        in_specs=[SMEM, SMEM, ANY, ANY, ANY, ANY],
        out_specs=VMEM,
        scratch_shapes=[
            pltpu.VMEM((toks, feats), bf),
            pltpu.VMEM((toks, HD), bf),
            pltpu.VMEM(out_weight.shape, bf),
            pltpu.VMEM((nz, toks, HD), bf),
            pltpu.VMEM((nz, HD, toks), bf),
            pltpu.VMEM((NX * PER, HD, feats), bf),
            pltpu.VMEM((NX * PER, HD + ONES, feats), f32),
            pltpu.VMEM((NX * PER, 1, feats), f32),
            pltpu.VMEM((NX - 1, parts, HD, feats // PARTS), bf),
            pltpu.VMEM((NX - 1, parts, HD, feats // PARTS), bf),
            pltpu.VMEM((NX - 1, parts, 1, feats // PARTS), f32),
            pltpu.VMEM((NX - 1, parts, 1, feats // PARTS), f32),
            pltpu.VMEM((toks, feats), bf),
            pltpu.VMEM((parts, ny, SUB, cols), bf),
            pltpu.VMEM((parts, ny, SUB, cols), bf),
            pltpu.VMEM((parts, ny - 1, SUB, cols), bf),
            pltpu.VMEM((parts, ny - 1, SUB, cols), bf),
            pltpu.VMEM((parts, SUB, cols), f32),
            dma((4,)), dma((2 * SPLIT, 2, nz // 2)), dma((2 * SPLIT, 2, nz // 2)),
            dma((NX - 1, PER)), dma((NX - 1, PER)),
            dma((NX - 1, parts)), dma((NX - 1, parts)), dma((NX - 1, parts)), dma((NX - 1, parts)),
            dma((parts, ny)), dma((parts, ny)), dma((parts, ny - 1)), dma((parts, ny - 1)),
        ],
        compiler_params=pltpu.CompilerParams(
            collective_id=0, has_side_effects=True, vmem_limit_bytes=56 << 20
        ),
        name="layer",
    )(swap_pairs, doc_blocks, queries, keys, values, out_weight)


def solution(mesh):
    nz = mesh.shape["ctx"] // NX
    ny = mesh.shape["head"] // NC
    in_specs = (P("ctx", "head"), P("ctx", "head"), P("ctx", "head"), P("head", None), P(), P())
    return jax.shard_map(
        functools.partial(local, nz=nz, ny=ny),
        mesh=mesh, in_specs=in_specs, out_specs=P("ctx", "head"), check_vma=False,
    )
```

```python
import functools

import jax
import jax.numpy as jnp
from jax import lax
from jax.experimental import pallas as pl
from jax.experimental.pallas import tpu as pltpu
from jax.sharding import PartitionSpec as P

HD = 128
BLOCK = 128
NX = 4
NC = 2
PER = 2
ONES = 16
SPLIT = 2
PARTS = 2
SUB = BLOCK // PARTS
MIRROR = (0, 2, 1, 3)
SCALE2 = 1.4426950408889634 * HD ** (-0.5)
MASKED = -1e30
MESH = pl.DeviceIdType.MESH
ANY = pl.BlockSpec(memory_space=pl.ANY)
VMEM = pl.BlockSpec(memory_space=pltpu.VMEM)
SMEM = pl.BlockSpec(memory_space=pltpu.SMEM)


def layer_kernel(
    nz, ny,
    swap, docs, q_ref, k_ref, v_ref, w_ref, out_ref,
    q_in, v_in, w_all, k_all, v_all, qt, acc, tops,
    o_give, o_take, s_give, s_take, att, given, taken, sums, finals, kept,
    lsem, zsend, zrecv, qsend, qrecv, osend, orecv, ssend, srecv, csend, crecv, ysend, yrecv,
):
    ctx = lax.axis_index("ctx")
    head = lax.axis_index("head")
    z, x = ctx // NX, lax.rem(ctx, NX)
    y, core = head // NC, lax.rem(head, NC)
    zat = lambda zz: lax.rem(zz + nz, nz)
    yat = lambda yy: lax.rem(yy + ny, ny)
    zdev = lambda d: (zat(z + d) * NX + x, head)
    columns = [x, lax.rem(x + 1, NX), lax.rem(x + NX - 1, NX), lax.rem(x + 2, NX)]
    peers = [(z * NX + c, head) for c in columns]
    twin = (ctx, y * NC + 1 - core)
    ydev = lambda yy: (ctx, yat(yy) * NC + core)
    hops = (2, 1, 3)
    far = nz // 2
    group = qt.shape[2] // BLOCK
    cols = out_ref.shape[1]

    def remote(src, dst, send_sem, recv_sem, device):
        return pltpu.make_async_remote_copy(
            src_ref=src, dst_ref=dst, send_sem=send_sem, recv_sem=recv_sem, device_id=device, device_id_type=MESH
        )

    barrier = pltpu.get_barrier_semaphore()
    friends = [zdev(d) for d in (1, -1)] + peers[1:] + [twin] + [ydev(y + d) for d in hops]
    for device in friends:
        pl.semaphore_signal(barrier, inc=1, device_id=device, device_id_type=MESH)

    loads = [
        pltpu.make_async_copy(q_ref, q_in, lsem.at[0]),
        pltpu.make_async_copy(v_ref, v_in, lsem.at[1]),
        pltpu.make_async_copy(k_ref, k_all.at[z], lsem.at[2]),
        pltpu.make_async_copy(w_ref, w_all, lsem.at[3]),
    ]
    for c in loads:
        c.start()
    loads[1].wait()
    v_all[z] = v_in[...].T
    loads[0].wait()
    for t in range(PER):
        for h in range(group):
            turned = q_in[t * BLOCK:(t + 1) * BLOCK, h * HD:(h + 1) * HD].T
            for u in range(PARTS):
                qt[t, :, (u * group + h) * SUB:(u * group + h + 1) * SUB] = turned[:, u * SUB:(u + 1) * SUB]
    loads[2].wait()
    pl.semaphore_wait(barrier, len(friends))

    def zcopy(stream, way, step):
        origin = zat(z - step) if way == 0 else zat(z + step)
        ref = k_all if stream < SPLIT else v_all
        size = ref.shape[1] // SPLIT
        ref = ref.at[origin, pl.ds(stream % SPLIT * size, size)]
        sems = (stream, way, step)
        return remote(ref, ref, zsend.at[sems], zrecv.at[sems], zdev(1 if way == 0 else -1))

    zall = [
        (stream, way, step)
        for step in range(far) for stream in range(2 * SPLIT) for way in (0, 1)
        if step < far - 1 or (stream < SPLIT) == (way == 0)
    ]
    zc = {key: zcopy(*key) for key in zall}
    pick = lambda step: [key for key in zall if key[2] == step]
    qcopy = [
        [
            remote(qt.at[t], qt.at[PER * MIRROR[p] + t], qsend.at[p - 1, t], qrecv.at[MIRROR[p] - 1, t], peers[p])
            for t in range(PER)
        ]
        for p in range(1, NX)
    ]
    for key in pick(0):
        zc[key].start()
    for p in (1, 2, 3):
        qcopy[p - 1][0].start()

    def arrive(step, streams=range(2 * SPLIT)):
        for key in pick(step):
            if key[0] not in streams:
                continue
            zc[key].wait_recv()
            onward = key[:2] + (step + 1,)
            if onward in zc:
                zc[onward].start()

    def queries(p, t):
        qcopy[MIRROR[p] - 1][t].wait_recv()

    seqs, starts = [], []
    for j in range(NX * PER):
        seq = swap[(z * NX + columns[j // PER]) * PER + j % PER]
        start = jnp.int32(0)
        end = jnp.int32(0)
        for d in range(docs.shape[0]):
            end = end + docs[d]
            start = jnp.where(end <= seq, end, start)
        seqs.append(seq)
        starts.append(start)

    acc[...] = jnp.zeros_like(acc)
    tops[...] = jnp.full_like(tops, MASKED)
    wide = group * SUB
    lane = lax.broadcasted_iota(jnp.int32, (BLOCK, PARTS * wide), 1)
    causal = lax.broadcasted_iota(jnp.int32, (BLOCK, PARTS * wide), 0) <= lane // wide * SUB + lax.rem(lane, SUB)

    def score(j, chunks, diagonal=False):
        rows, offsets = [], []
        new = tops[j]
        for origin in chunks:
            s = jnp.dot(k_all[origin], qt[j], preferred_element_type=jnp.float32)
            for b in range(PER):
                ks = swap[(origin * NX + x) * PER + b]
                seen = (ks >= starts[j]) & (ks <= seqs[j])
                offset = jnp.where(seen, 0.0, MASKED).astype(jnp.float32)
                part = s[b * BLOCK:(b + 1) * BLOCK]
                if diagonal and b == j:
                    part = jnp.where(causal, part, MASKED)
                new = jnp.maximum(new, jnp.max(part, axis=0, keepdims=True) + offset)
                rows.append(part)
                offsets.append(offset)
        return j, chunks, rows, offsets, new

    def absorb(j, chunks, rows, offsets, new):
        level = new * SCALE2
        weights = [
            jnp.exp2(part * SCALE2 - (level - offset)).astype(jnp.bfloat16) for part, offset in zip(rows, offsets)
        ]
        vals = jnp.concatenate([v_all[origin] for origin in chunks], axis=1)
        vals = jnp.concatenate([vals, jnp.ones((ONES, vals.shape[1]), jnp.bfloat16)], axis=0)
        product = jnp.dot(vals, jnp.concatenate(weights, axis=0), preferred_element_type=jnp.float32)
        acc[j] = acc[j] * jnp.exp2((tops[j] - new) * SCALE2) + product
        tops[j] = new

    def attend(units, done=lambda p, t: None):
        ask = lambda p, t, rows: score(PER * p + t, [c for r in rows for c in row(r)])
        asked = ask(*units[0])
        for n, (p, t, _) in enumerate(units):
            ahead = ask(*units[n + 1]) if n + 1 < len(units) else None
            absorb(*asked)
            done(p, t)
            asked = ahead

    def row(step):
        if step < 0:
            return [z]
        return [zat(z - 1 - step), zat(z + 1 + step)] if step < far - 1 else [zat(z + far)]

    pieces = [(t, u) for t in range(PER) for u in range(PARTS)]

    def back(give_ref, take_ref, sends, recvs, p, i):
        m = MIRROR[p] - 1
        return remote(
            give_ref.at[p - 1, i], take_ref.at[m, i], sends.at[p - 1, i], recvs.at[m, i], peers[p]
        )

    ocopy = [[back(o_give, o_take, osend, orecv, p, i) for i in range(len(pieces))] for p in range(1, NX)]
    scopy = [[back(s_give, s_take, ssend, srecv, p, i) for i in range(len(pieces))] for p in range(1, NX)]

    def give(p, i):
        t, u = pieces[i]
        j = PER * p + t
        lanes = slice(u * wide, (u + 1) * wide)
        total = acc[j, HD:HD + 1, lanes]
        some = total > 0.0
        total = jnp.where(some, total, 1.0)
        s_give[p - 1, i] = jnp.where(some, tops[j, :, lanes] * SCALE2 + jnp.log2(total), MASKED)
        o_give[p - 1, i] = (acc[j, :HD, lanes] / total).astype(jnp.bfloat16)
        scopy[p - 1][i].start()
        ocopy[p - 1][i].start()

    def product(i, yy, cc):
        at = pl.multiple_of((yat(yy) * NC + cc) * cols, cols)
        return jnp.dot(att[i * SUB:(i + 1) * SUB, :], w_all[:, pl.ds(at, cols)], preferred_element_type=jnp.float32)

    order = hops + (0,)
    ccopy = [
        [remote(given.at[i, n], taken.at[i, n], csend.at[i, n], crecv.at[i, n], twin) for n in range(ny)]
        for i in range(len(pieces))
    ]
    ycopy = [
        [
            remote(sums.at[i, n], finals.at[i, n], ysend.at[i, n], yrecv.at[i, n], ydev(y + d))
            for n, d in enumerate(hops)
        ]
        for i in range(len(pieces))
    ]

    def merge(i):
        t, u = pieces[i]
        lanes = slice(u * wide, (u + 1) * wide)
        for p in range(NX - 1):
            scopy[p][i].wait_recv()
            ocopy[p][i].wait_recv()
        own_level = tops[t, :, lanes] * SCALE2
        levels = [own_level + jnp.log2(acc[t, HD:HD + 1, lanes])] + [s_take[p, i] for p in range(NX - 1)]
        top = functools.reduce(jnp.maximum, levels)
        shares = [jnp.exp2(v - top) for v in levels]
        whole = functools.reduce(jnp.add, shares)
        mixed = acc[t, :HD, lanes] * (jnp.exp2(own_level - top) / whole)
        for p in range(NX - 1):
            mixed = mixed + o_take[p, i].astype(jnp.float32) * (shares[p + 1] / whole)
        for h in range(group):
            att[i * SUB:(i + 1) * SUB, h * HD:(h + 1) * HD] = (
                mixed[:, h * SUB:(h + 1) * SUB].T.astype(jnp.bfloat16)
            )
        for n, d in enumerate(order):
            given[i, n] = product(i, y + d, 1 - core).astype(jnp.bfloat16)
            ccopy[i][n].start()

    def scatter(i):
        for n, d in enumerate(order):
            total = product(i, y + d, core)
            ccopy[i][n].wait_recv()
            total = total + taken[i, n].astype(jnp.float32)
            if d:
                sums[i, n] = total.astype(jnp.bfloat16)
                ycopy[i][n].start()
            else:
                kept[i] = total

    def finish(i):
        total = kept[i]
        for n in range(len(hops)):
            ycopy[i][n].wait_recv()
            total = total + finals[i, n].astype(jnp.float32)
        out_ref[i * SUB:(i + 1) * SUB, :] = total.astype(out_ref.dtype)

    last = far - 1
    table = [
        [(0, 0, [0]), (0, 1, [0])],
        [(1, 0, [-1, 0, 1]), (2, 0, [-1, 0, 1]), (0, 0, [1])],
        [(3, 0, [-1, 0, 1, 2]), (1, 1, [-1, 0, 1, 2]), (2, 1, [-1, 0, 1, 2])],
        [(3, 1, [-1, 0, 1, 2, 3]), (0, 0, [2, 3]), (0, 1, [1, 2, 3])],
        [(1, 0, [2, 3, 4]), (2, 0, [2, 3, 4]), (3, 0, [3, 4])],
        [(1, 1, [3, 4, 5]), (2, 1, [3, 4, 5]), (3, 1, [4, 5]), (0, 1, [4, 5])],
        [(3, 0, [5, 6]), (1, 0, [5, 6]), (2, 0, [5, 6]), (0, 0, [4, 5, 6])],
    ]
    for t in range(PER):
        absorb(*score(t, [z], diagonal=True))

    def second_half(p):
        qcopy[p - 1][0].wait_send()
        qcopy[p - 1][1].start()

    second_half(1)
    second_half(2)
    asked = set()
    for step, units in enumerate(table):
        arrive(step)
        if step == 0:
            second_half(3)
        for p, t, _ in units:
            if p and (p, t) not in asked:
                queries(p, t)
                asked.add((p, t))
        attend(units)
    arrive(last)

    def done(p, t):
        if p and t == 0:
            for u in range(PARTS):
                give(p, u)
        elif p:
            give(p, PARTS)
        if (p, t) == (2, 1):
            for u in range(1, PARTS):
                for peer in (3, 1, 2):
                    give(peer, PARTS + u)

    ends = [(p, 0, [last]) for p in (3, 1, 2, 0)] + [(p, 1, [last - 1, last]) for p in (3, 1, 2, 0)]
    attend(ends, done)
    loads[3].wait()
    for i in range(len(pieces)):
        merge(i)
        if i:
            scatter(i - 1)
    scatter(len(pieces) - 1)
    for i in range(len(pieces)):
        finish(i)

    for c in [copies[1] for copies in qcopy]:
        c.wait_send()
    for copies in ocopy + scopy + ccopy + ycopy:
        for c in copies:
            c.wait_send()
    for key in zall:
        zc[key].wait_send()


def local(queries, keys, values, out_weight, doc_blocks, swap_pairs, nz, ny):
    toks, feats = queries.shape
    dma = pltpu.SemaphoreType.DMA
    bf = jnp.bfloat16
    f32 = jnp.float32
    cols = out_weight.shape[1] // (ny * NC)
    parts = PER * PARTS
    return pl.pallas_call(
        functools.partial(layer_kernel, nz, ny),
        out_shape=jax.ShapeDtypeStruct((toks, cols), bf),
        in_specs=[SMEM, SMEM, ANY, ANY, ANY, ANY],
        out_specs=VMEM,
        scratch_shapes=[
            pltpu.VMEM((toks, feats), bf),
            pltpu.VMEM((toks, HD), bf),
            pltpu.VMEM(out_weight.shape, bf),
            pltpu.VMEM((nz, toks, HD), bf),
            pltpu.VMEM((nz, HD, toks), bf),
            pltpu.VMEM((NX * PER, HD, feats), bf),
            pltpu.VMEM((NX * PER, HD + ONES, feats), f32),
            pltpu.VMEM((NX * PER, 1, feats), f32),
            pltpu.VMEM((NX - 1, parts, HD, feats // PARTS), bf),
            pltpu.VMEM((NX - 1, parts, HD, feats // PARTS), bf),
            pltpu.VMEM((NX - 1, parts, 1, feats // PARTS), f32),
            pltpu.VMEM((NX - 1, parts, 1, feats // PARTS), f32),
            pltpu.VMEM((toks, feats), bf),
            pltpu.VMEM((parts, ny, SUB, cols), bf),
            pltpu.VMEM((parts, ny, SUB, cols), bf),
            pltpu.VMEM((parts, ny - 1, SUB, cols), bf),
            pltpu.VMEM((parts, ny - 1, SUB, cols), bf),
            pltpu.VMEM((parts, SUB, cols), f32),
            dma((4,)), dma((2 * SPLIT, 2, nz // 2)), dma((2 * SPLIT, 2, nz // 2)),
            dma((NX - 1, PER)), dma((NX - 1, PER)),
            dma((NX - 1, parts)), dma((NX - 1, parts)), dma((NX - 1, parts)), dma((NX - 1, parts)),
            dma((parts, ny)), dma((parts, ny)), dma((parts, ny - 1)), dma((parts, ny - 1)),
        ],
        compiler_params=pltpu.CompilerParams(
            collective_id=0, has_side_effects=True, vmem_limit_bytes=56 << 20
        ),
        name="layer",
    )(swap_pairs, doc_blocks, queries, keys, values, out_weight)


def solution(mesh):
    nz = mesh.shape["ctx"] // NX
    ny = mesh.shape["head"] // NC
    in_specs = (P("ctx", "head"), P("ctx", "head"), P("ctx", "head"), P("head", None), P(), P())
    return jax.shard_map(
        functools.partial(local, nz=nz, ny=ny),
        mesh=mesh, in_specs=in_specs, out_specs=P("ctx", "head"), check_vma=False,
    )
```
